256 devices in a mesh: prow: 16 (over z_hi, y, core), pcol: 16 (over x, z_lo).
Axes of the slice: x: 4, y: 4, z: 8 (z_hi: 2, z_lo: 4; z = z_hi * 4 + z_lo), core: 2. Of those that a mesh axis runs over, the one named last changes fastest.
Arguments:
- coords: float32 [2, 8, 8192], P(None, None, 'prow'), may hold values from 0 to 1
- observations: float32 [8, 8192], P(None, 'prow'), may hold values from -6 to 6
- length_scale: float32 [1], replicated, may hold values from 0.06 to 0.15
- nugget: float32 [1], replicated, may hold values from 0.3 to 1
Outputs:
- slab: float32 [8, 8192, 2048], P(None, 'prow', 'pcol')
- whitened: float32 [8, 8192], P(None, 'prow')
- loglik_part: float32 [1], replicated
The draws below stay inside these ranges and needn't reach their ends.
All inputs are finite; a program needn't handle non-finite values.
Results may differ from the reference program's by a relative error of at most 0.0003.
Values sent between devices are 32-bit elements; how exact they have to be, the bound alone decides.
A program may use at most 128 MiB of HBM per device.

```python
import math
import jax
import jax.numpy as jnp
from jax import lax

B = 512
RT_DEV = 8
SLAB = 2048
N_PROW = 16


def shard_levels(rng, shape, pieces, low, high):
    def one(dim, blocks):
        steps = jax.random.uniform(jax.random.fold_in(jax.random.fold_in(rng, 6), dim), (blocks,), jnp.float32, low / len(pieces), high / len(pieces))
        return jnp.repeat(jnp.exp(steps), shape[dim] // blocks).reshape((-1,) + (1,) * (len(shape) - dim - 1))

    level = one(*pieces[0])
    for cut in pieces[1:]:
        level = level * one(*cut)
    return level


def centred(key, dims, width, reach, split=(), kind=jnp.bfloat16):
    array = width * jax.random.normal(key, dims, jnp.float32)
    if split:
        array = array * shard_levels(key, dims, split, -0.22, 0.18)
    return jnp.clip(array, -reach, reach).astype(kind)


def setup_inputs(seed: int = 0) -> dict:
    seeds = jax.random.split(jax.random.key(seed), 5)
    return {
        "coords": jnp.clip(1.0 * jax.random.uniform(seeds[0], (2, RT_DEV, N_PROW * B), jnp.float32) ** shard_levels(seeds[0], (2, RT_DEV, N_PROW * B), ((2, 16),), -0.2, 0.2), 0.0, 1.0),
        "observations": centred(seeds[1], (RT_DEV, N_PROW * B), 1.0, 6.0, ((1, 16),), jnp.float32),
        "length_scale": jnp.clip(jax.random.uniform(seeds[2], (1,), jnp.float32, 0.06, 0.15), 0.06, 0.15),
        "nugget": jnp.clip(jax.random.uniform(seeds[3], (1,), jnp.float32, 0.3, 1.0), 0.3, 1.0),
    }


def matern_block(left_x, left_y, right_x, right_y, decay_rate):
    delta_x = left_x[:, None] - right_x[None, :]
    delta_y = left_y[:, None] - right_y[None, :]
    scaled = decay_rate * jnp.sqrt(delta_x * delta_x + delta_y * delta_y)
    return (1.0 + scaled) * jnp.exp(-scaled)

def transposed_product(left, right):
    return jnp.dot(left.astype(jnp.float32), right.T.astype(jnp.float32), precision=lax.Precision.HIGHEST, preferred_element_type=jnp.float32)

def reference(coords, observations, length_scale, nugget):
    flat_x = coords[0].reshape(-1)
    flat_y = coords[1].reshape(-1)
    values = observations.reshape(-1)
    count = flat_x.shape[0]
    decay_rate = math.sqrt(3.0) / length_scale[0]
    nugget_value = nugget[0]
    site_ids = jnp.arange(count, dtype=jnp.int32)

    def covariance(row_lo, row_hi, col_lo, col_hi):
        rows = site_ids[row_lo:row_hi]
        cols = site_ids[col_lo:col_hi]
        same = (rows[:, None] == cols[None, :]).astype(jnp.float32)
        return matern_block(flat_x[row_lo:row_hi], flat_y[row_lo:row_hi], flat_x[col_lo:col_hi], flat_y[col_lo:col_hi], decay_rate) + nugget_value * same
    identity = jnp.eye(B, dtype=jnp.float32)
    cov_first = covariance(0, count, 0, B)
    factor_first = jnp.linalg.cholesky(cov_first[:B])
    inverse_first = jax.scipy.linalg.solve_triangular(factor_first, identity, lower=True)
    panel_first = transposed_product(cov_first, inverse_first)
    panel_first = panel_first.at[:B].set(factor_first)
    cov_second = covariance(0, count, B, 2 * B)
    schur_second = cov_second - transposed_product(panel_first, panel_first[B:2 * B])
    factor_second = jnp.linalg.cholesky(schur_second[B:2 * B])
    inverse_second = jax.scipy.linalg.solve_triangular(factor_second, identity, lower=True)
    panel_second = transposed_product(schur_second, inverse_second)
    panel_second = panel_second.at[:B].set(0.0).at[B:2 * B].set(factor_second)
    slab_lo = 2 * B
    slab_hi = 2 * B + SLAB
    cov_slab = covariance(0, count, slab_lo, slab_hi)
    slab = cov_slab - transposed_product(panel_first, panel_first[slab_lo:slab_hi]) - transposed_product(panel_second, panel_second[slab_lo:slab_hi])
    slab = jnp.where((site_ids < 2 * B)[:, None], 0.0, slab)
    hp = lax.Precision.HIGHEST
    whitened_first = jnp.dot(inverse_first, values[:B], precision=hp)
    whitened_second = jnp.dot(inverse_second, values[B:2 * B] - jnp.dot(panel_first[B:2 * B], whitened_first, precision=hp), precision=hp)
    whitened = values - jnp.dot(panel_first, whitened_first, precision=hp) - jnp.dot(panel_second, whitened_second, precision=hp)
    whitened = whitened.at[:B].set(whitened_first).at[B:2 * B].set(whitened_second)
    quadratic = 0.5 * (jnp.sum(whitened_first * whitened_first) + jnp.sum(whitened_second * whitened_second))
    log_terms = jnp.sum(jnp.log(jnp.diagonal(factor_first))) + jnp.sum(jnp.log(jnp.diagonal(factor_second)))
    loglik_part = -(quadratic + log_terms) / (2.0 * B)
    return (slab.reshape(RT_DEV, N_PROW * B, SLAB), whitened.reshape(RT_DEV, N_PROW * B), loglik_part.reshape(1))
```

```python
import math

import jax
import jax.numpy as jnp
from jax import lax
from jax.experimental import pallas as pl
from jax.experimental.pallas import tpu as pltpu
from jax.sharding import PartitionSpec as P

SQRT_THREE = math.sqrt(3.0)
F32 = jnp.float32
BF16 = jnp.bfloat16
MESH = pl.DeviceIdType.MESH

B = 512
T = 2 * B
NB = 128
NK = T // NB
N_PROW = 16
TILES = 8
NC = 128
WIDTH = T + 2 * NC


def gather_kernel(pk_ref, t_ref, c_ref, t0, t1, tc, send_sem, recv_sem):
    prow = lax.axis_index("prow")
    pcol = lax.axis_index("pcol")
    col_owner = 2 + pcol // 4
    part = pl.ds(pl.multiple_of((pcol % 4) * NC, NC), NC)
    barrier = pltpu.get_barrier_semaphore()
    senders = ((0, 0), (1, 1), (col_owner, 2))
    for owner, _ in senders:
        @pl.when(prow != owner)
        def _():
            pl.semaphore_signal(barrier, inc=1, device_id=(owner, pcol), device_id_type=MESH)

    sources = (pk_ref, pk_ref, pk_ref.at[:, part])
    slots = (t0, t1, tc)

    def copy(slot, step, target):
        return pltpu.make_async_remote_copy(
            src_ref=sources[slot], dst_ref=slots[slot],
            send_sem=send_sem.at[step], recv_sem=recv_sem.at[slot],
            device_id=(target, pcol), device_id_type=MESH)

    for owner, slot in senders:
        @pl.when(prow == owner)
        def _():
            pl.semaphore_wait(barrier, N_PROW - 1)
            for step in range(1, N_PROW):
                copy(slot, step, (prow + step) % N_PROW).start()
            slots[slot][...] = sources[slot][...]
            for step in range(1, N_PROW):
                copy(slot, step, (prow + step) % N_PROW).wait_send()
    for owner, slot in senders:
        @pl.when(prow != owner)
        def _():
            copy(slot, 1, (prow + 1) % N_PROW).wait_recv()
    t_ref[:, :B] = t0[...]
    t_ref[:, B:] = t1[...]
    c_ref[...] = tc[...]


def gather_sites(pk):
    vm = pl.BlockSpec(memory_space=pltpu.VMEM)
    return pl.pallas_call(
        gather_kernel,
        out_shape=(jax.ShapeDtypeStruct((4, T), F32), jax.ShapeDtypeStruct((4, NC), F32)),
        in_specs=[vm], out_specs=(vm, vm),
        scratch_shapes=[
            pltpu.VMEM((4, B), F32), pltpu.VMEM((4, B), F32), pltpu.VMEM((4, NC), F32),
            pltpu.SemaphoreType.DMA((N_PROW,)), pltpu.SemaphoreType.DMA((3,)),
        ],
        compiler_params=pltpu.CompilerParams(collective_id=0, has_side_effects=True),
        name="gather_sites",
    )(pk)


def split(x):
    high = x.astype(BF16)
    return high, (x - high.astype(F32)).astype(BF16)


def matern(dx, dy):
    q = jnp.maximum(dx * dx + dy * dy, 1e-30)
    s = q * lax.rsqrt(q)
    return (1.0 + s) * jnp.exp(-s)


def lanes(x, j):
    return jnp.broadcast_to(x[:, j:j + 1], (8, 128))


def rows(x, i):
    return jnp.broadcast_to(x[i:i + 1, :], (8, 128))


def mm(x, y):
    return lax.dot_general(x, y, (((1,), (0,)), ((), ())), preferred_element_type=F32)


def mm3(x, y):
    xh, xl = split(x)
    yh, yl = split(y)
    return mm(jnp.concatenate([xh, xh, xl], 1), jnp.concatenate([yh, yl, yh], 0))


def factor_block(load, store):
    lane = lax.broadcasted_iota(jnp.int32, (8, 128), 1)
    sub = lax.broadcasted_iota(jnp.int32, (8, 128), 0)
    a = [load(i) for i in range(16)]
    pivots = jnp.ones((8, 128), F32)
    for b in range(16):
        w_out = jnp.zeros((8, 128), F32)
        for h in range(2):
            j0 = 8 * b + 4 * h
            pivot_lanes = (lane >= j0) & (lane < j0 + 4)
            eye = (lane - j0) == (sub - 4 * h)
            r = a[b]
            cb = [lanes(r, j0 + t) for t in range(4)]
            s = {(i, t): rows(cb[t], 4 * h + i) for t in range(4) for i in range(t, 4)}
            rpp = jnp.where(pivot_lanes, jnp.where(eye, 1.0, 0.0), r)
            rb = [rows(rpp, 4 * h + t) for t in range(4)]
            rp = []
            l = {}
            for t in range(4):
                rp.append(1.0 / s[t, t])
                for i in range(t + 1, 4):
                    l[i, t] = s[i, t] * rp[t]
                for i in range(t + 1, 4):
                    for c in range(t + 1, i + 1):
                        s[i, c] = s[i, c] - l[i, t] * s[c, t]
                    rb[i] = rb[i] - l[i, t] * rb[t]
            for t in range(4):
                pivots = jnp.where(lane == j0 + t, s[t, t], pivots)
                w = jnp.where(lane < j0 + 4, rb[t] * lax.rsqrt(s[t, t]), 0.0)
                w_out = jnp.where(sub == 4 * h + t, w, w_out)
            x = [None] * 4
            for t in (3, 2, 1, 0):
                x[t] = rb[t] * rp[t]
                for i in range(t + 1, 4):
                    x[t] = x[t] - l[i, t] * x[i]
            for i in range(b if h == 0 else b + 1, 16):
                c = cb if i == b else [lanes(a[i], j0 + t) for t in range(4)]
                new = jnp.where(pivot_lanes, 0.0, a[i]) - (
                    (c[0] * x[0] + c[1] * x[1]) + (c[2] * x[2] + c[3] * x[3]))
                a[i] = jnp.where(sub >= 4, new, a[i]) if i == b else new
        store(b, w_out)
    return pivots


def main_kernel(ls_ref, ng_ref, co_ref, ob_ref, t_ref, c_ref,
                slab_ref, white_ref, ll_ref,
                a_ref, w_ref, wt_ref, yh_ref, yl_ref, yb_ref, z_ref, m_ref,
                rx_ref, ry_ref, mc_ref, wv_ref, ld_ref, flat_ref):
    prow = lax.axis_index("prow")
    pcol = lax.axis_index("pcol")
    rate = SQRT_THREE / jnp.full((1, 128), ls_ref[0], F32)
    nugget = ng_ref[0]
    lane = lax.broadcasted_iota(jnp.int32, (8, 128), 1)
    sub = lax.broadcasted_iota(jnp.int32, (8, 128), 0)
    rate_t = jnp.concatenate([rate] * 8, 1)
    tx = t_ref[0:1, :] * rate_t
    ty = t_ref[1:2, :] * rate_t
    cx = c_ref[0:1, :] * rate
    cy = c_ref[1:2, :] * rate
    ux = [tx[:, 128 * i:128 * i + 128] for i in range(8)] + [cx]
    uy = [ty[:, 128 * i:128 * i + 128] for i in range(8)] + [cy]

    for q in range(TILES):
        for i in range(4):
            part = slice(128 * i, 128 * i + 128)
            at = slice(q * B + 128 * i, q * B + 128 * i + 128)
            rx_ref[at, :] = jnp.broadcast_to(co_ref[0, q:q + 1, part] * rate, (128, 128)).T
            ry_ref[at, :] = jnp.broadcast_to(co_ref[1, q:q + 1, part] * rate, (128, 128)).T
            flat_ref[4 * q + i:4 * q + i + 1, :] = ob_ref[q:q + 1, part]

    for k in range(NK):
        part = slice(128 * k, 128 * k + 128)
        px = jnp.broadcast_to(tx[:, part], (128, 128)).T
        py = jnp.broadcast_to(ty[:, part], (128, 128)).T
        w_ref[0] = px
        w_ref[1] = py
        wide = lax.broadcasted_iota(jnp.int32, (128, 128), 1)
        a_ref[k, :, T + NC:] = jnp.where(
            wide == 0, jnp.broadcast_to(t_ref[2:3, part], (128, 128)).T, 0.0)

        def build(g, carry, k=k):
            at = pl.ds(pl.multiple_of(8 * g, 8), 8)
            gx = w_ref[0, at, :]
            gy = w_ref[1, at, :]
            for j in range(k, 9):
                v = matern(gx - ux[j], gy - uy[j])
                if j == k:
                    v = v + jnp.where(lane == sub + 8 * g, nugget, 0.0)
                a_ref[k, at, 128 * j:128 * j + 128] = v
            return carry
        lax.fori_loop(0, 16, build, 0)

    ld_ref[...] = jnp.zeros((8, 128), F32)

    def step(k, carry):
        off = pl.ds(pl.multiple_of(128 * k, 128), 128)

        def load(i):
            return a_ref[k, 8 * i:8 * i + 8, off]

        def store(i, w):
            w_ref[k, 8 * i:8 * i + 8, :] = w

        pivots = factor_block(load, store)
        ld_ref[...] = ld_ref[...] + jnp.log(pivots)
        for kk in range(NK):
            @pl.when(k == kk)
            def _():
                o = 128 * (kk + 1)
                n = WIDTH - o
                w = w_ref[kk]
                wt_ref[kk] = w.T
                y = mm3(w, a_ref[kk, :, o:])
                yh, yl = split(y)
                if kk < NK - 1:
                    yh_ref[kk, :, o:T] = yh[:, :n - 256]
                    yl_ref[kk, :, o:T] = yl[:, :n - 256]
                yb_ref[kk] = y[:, n - 256:]
                z_ref[kk:kk + 1, :] = y[:, n - 128:].T[0:1, :]
                ycat = jnp.concatenate([yh, yl, yh], 0)
                for i in range(kk + 1, NK):
                    f = 128 * (i - kk - 1)
                    th, tl = split(y[:, f:f + 128].T)
                    tcat = jnp.concatenate([th, th, tl], 1)
                    a_ref[i, :, 128 * i:] = a_ref[i, :, 128 * i:] - mm(tcat, ycat[:, f:])
        return carry
    lax.fori_loop(0, NK, step, 0)

    for k in range(NK - 1, -1, -1):
        acc = yb_ref[k]
        if k < NK - 1:
            o = 128 * (k + 1)
            mh, ml = split(m_ref[o:, :])
            yh = yh_ref[k, :, o:T]
            acc = acc - (mm(yh, mh) + mm(yh, ml) + mm(yl_ref[k, :, o:T], mh))
        m_ref[128 * k:128 * k + 128, :] = mm3(wt_ref[k], acc)

    mh, ml = split(m_ref[:, :NC])
    mc_ref[:, :NC] = mh
    mc_ref[:, NC:] = ml
    wt = m_ref[:, NC:].T
    wh, wl = split(wt[0:1, :])
    wv_ref[...] = jnp.concatenate([wh, wl, jnp.zeros((14, T), BF16)], 0)

    z = z_ref[...]
    total = jnp.sum(z * z) + jnp.sum(ld_ref[0:1, :])
    ll_ref[...] = jnp.full((1, 128), total * (-0.5 / T), F32)

    def body(r, carry):
        q = r // 4
        j = r % 4
        at = pl.ds(pl.multiple_of(128 * r, 128), 128)
        gx = rx_ref[at, :]
        gy = ry_ref[at, :]
        acc = None
        for t in range(4):
            piece = jnp.concatenate(
                [matern(gx - ux[2 * t + e], gy - uy[2 * t + e]) for e in range(2)], 1)
            ch, cl = split(piece)
            mt = mc_ref[256 * t:256 * t + 256, :]
            wv = wv_ref[:, 256 * t:256 * t + 256]
            both = mm(ch, mt)
            low = mm(cl, mt[:, :NC])
            wr = lax.dot_general(wv, ch, (((1,), (1,)), ((), ())), preferred_element_type=F32)
            wr2 = lax.dot_general(wv, cl, (((1,), (1,)), ((), ())), preferred_element_type=F32)
            cur = (both[:, :NC] + both[:, NC:] + low, wr[0:1] + wr[1:2] + wr2[0:1])
            acc = cur if acc is None else (acc[0] + cur[0], acc[1] + cur[1])
        panel = (q == 0) & (prow < 2)
        first = (q * N_PROW + prow) * B + 128 * j - (T + pcol * NC)
        wl_ = lax.broadcasted_iota(jnp.int32, (128, 128), 1)
        ws_ = lax.broadcasted_iota(jnp.int32, (128, 128), 0)
        value = matern(gx - cx, gy - cy) + jnp.where(wl_ == ws_ + first, nugget, 0.0) - acc[0]
        slab_ref[q, pl.ds(pl.multiple_of(128 * j, 128), 128), :] = jnp.where(panel, 0.0, value)
        zr = z_ref[pl.ds(jnp.minimum(prow, 1) * 4 + j, 1), :]
        flat_ref[pl.ds(r, 1), :] = jnp.where(panel, zr, flat_ref[pl.ds(r, 1), :] - acc[1])
        return carry
    lax.fori_loop(0, 32, body, 0)
    for r in range(32):
        white_ref[r // 4:r // 4 + 1, 128 * (r % 4):128 * (r % 4) + 128] = flat_ref[r:r + 1, :]


def main_call(length_scale, nugget, coords, observations, sites, columns):
    vm = pl.BlockSpec(memory_space=pltpu.VMEM)
    sm = pl.BlockSpec(memory_space=pltpu.SMEM)
    return pl.pallas_call(
        main_kernel,
        out_shape=(jax.ShapeDtypeStruct((TILES, B, NC), F32),
                   jax.ShapeDtypeStruct((TILES, B), F32),
                   jax.ShapeDtypeStruct((1, 128), F32)),
        in_specs=[sm, sm, vm, vm, vm, vm], out_specs=(vm, vm, vm),
        scratch_shapes=[
            pltpu.VMEM((NK, NB, WIDTH), F32),
            pltpu.VMEM((NK, NB, NB), F32),
            pltpu.VMEM((NK, NB, NB), F32),
            pltpu.VMEM((NK, NB, T), BF16),
            pltpu.VMEM((NK, NB, T), BF16),
            pltpu.VMEM((NK, NB, 2 * NC), F32),
            pltpu.VMEM((NK, NB), F32),
            pltpu.VMEM((T, 2 * NC), F32),
            pltpu.VMEM((TILES * B, 128), F32),
            pltpu.VMEM((TILES * B, 128), F32),
            pltpu.VMEM((T, 2 * NC), BF16),
            pltpu.VMEM((16, T), BF16),
            pltpu.VMEM((8, 128), F32),
            pltpu.VMEM((32, 128), F32),
        ],
        compiler_params=pltpu.CompilerParams(vmem_limit_bytes=60 * 1024 * 1024),
        name="factor_and_slab",
    )(length_scale, nugget, coords, observations, sites, columns)


def shards(coords, observations, length_scale, nugget):
    pk = jnp.concatenate([coords[:, 0, :], observations[0:1], observations[0:1]], 0)
    sites, columns = gather_sites(pk)
    slab, white, ll = main_call(length_scale, nugget, coords, observations, sites, columns)
    return slab, white, ll[0, :1]


def solution(mesh):
    placed = (P(None, None, "prow"), P(None, "prow"), P(), P())
    return jax.shard_map(
        shards,
        mesh=mesh,
        in_specs=placed,
        out_specs=(P(None, "prow", "pcol"), P(None, "prow"), P()),
        check_vma=False,
    )
```

```python
import math

import jax
import jax.numpy as jnp
from jax import lax
from jax.experimental import pallas as pl
from jax.experimental.pallas import tpu as pltpu
from jax.sharding import PartitionSpec as P

SQRT_THREE = math.sqrt(3.0)
MINUS_LOG2E = -math.log2(math.e)
F32 = jnp.float32
BF16 = jnp.bfloat16
MESH = pl.DeviceIdType.MESH

B = 512
T = 2 * B
NB = 128
NK = T // NB
N_PROW = 16
TILES = 8
NC = 128
WIDTH = T + 2 * NC


def gather_kernel(pk_ref, t_ref, c_ref, t0, t1, tc, send_sem, recv_sem):
    prow = lax.axis_index("prow")
    pcol = lax.axis_index("pcol")
    col_owner = 2 + pcol // 4
    part = pl.ds(pl.multiple_of((pcol % 4) * NC, NC), NC)
    barrier = pltpu.get_barrier_semaphore()
    senders = ((0, 0), (1, 1), (col_owner, 2))
    for owner, _ in senders:
        @pl.when(prow != owner)
        def _():
            pl.semaphore_signal(barrier, inc=1, device_id=(owner, pcol), device_id_type=MESH)

    sources = (pk_ref, pk_ref, pk_ref.at[:, part])
    slots = (t0, t1, tc)

    def copy(slot, step, target):
        return pltpu.make_async_remote_copy(
            src_ref=sources[slot], dst_ref=slots[slot],
            send_sem=send_sem.at[step], recv_sem=recv_sem.at[slot],
            device_id=(target, pcol), device_id_type=MESH)

    for owner, slot in senders:
        @pl.when(prow == owner)
        def _():
            pl.semaphore_wait(barrier, N_PROW - 1)
            for step in range(1, N_PROW):
                copy(slot, step, (prow + step) % N_PROW).start()
            slots[slot][...] = sources[slot][...]
            for step in range(1, N_PROW):
                copy(slot, step, (prow + step) % N_PROW).wait_send()
    for owner, slot in senders:
        @pl.when(prow != owner)
        def _():
            copy(slot, 1, (prow + 1) % N_PROW).wait_recv()
    t_ref[:, :B] = t0[...]
    t_ref[:, B:] = t1[...]
    c_ref[...] = tc[...]


def gather_sites(pk):
    vm = pl.BlockSpec(memory_space=pltpu.VMEM)
    return pl.pallas_call(
        gather_kernel,
        out_shape=(jax.ShapeDtypeStruct((4, T), F32), jax.ShapeDtypeStruct((4, NC), F32)),
        in_specs=[vm], out_specs=(vm, vm),
        scratch_shapes=[
            pltpu.VMEM((4, B), F32), pltpu.VMEM((4, B), F32), pltpu.VMEM((4, NC), F32),
            pltpu.SemaphoreType.DMA((N_PROW,)), pltpu.SemaphoreType.DMA((3,)),
        ],
        compiler_params=pltpu.CompilerParams(collective_id=0, has_side_effects=True),
        name="gather_sites",
    )(pk)


def split(x):
    high = x.astype(BF16)
    return high, (x - high.astype(F32)).astype(BF16)


def matern(dx, dy):
    s = 1.0 / lax.rsqrt(dx * dx + dy * dy)
    return (1.0 + s) * jnp.exp2(s * MINUS_LOG2E)


def lanes(x, j):
    return jnp.broadcast_to(x[:, j:j + 1], (8, 128))


def rows(x, i):
    return jnp.take_along_axis(x, jnp.full((8, 128), i, jnp.int32), axis=0)


def mm(x, y):
    return lax.dot_general(x, y, (((1,), (0,)), ((), ())), preferred_element_type=F32)


def mm3(x, y):
    xh, xl = split(x)
    yh, yl = split(y)
    return mm(jnp.concatenate([xh, xh, xl], 1), jnp.concatenate([yh, yl, yh], 0))


def factor_block(load, store):
    lane = lax.broadcasted_iota(jnp.int32, (8, 128), 1)
    sub = lax.broadcasted_iota(jnp.int32, (8, 128), 0)
    a = [load(i) for i in range(16)]
    pivots = jnp.ones((8, 128), F32)
    for b in range(16):
        w_out = jnp.zeros((8, 128), F32)
        for h in range(2):
            j0 = 8 * b + 4 * h
            pivot_lanes = (lane >= j0) & (lane < j0 + 4)
            eye = (lane - j0) == (sub - 4 * h)
            r = a[b]
            cb = [lanes(r, j0 + t) for t in range(4)]
            s = {(i, t): rows(cb[t], 4 * h + i) for t in range(4) for i in range(t, 4)}
            rpp = jnp.where(pivot_lanes, jnp.where(eye, 1.0, 0.0), r)
            rb = [rows(rpp, 4 * h + t) for t in range(4)]
            nx = b if h == 0 else b + 1
            if h == 0:
                cn = [jnp.where(sub >= 4, c, 0.0) for c in cb]
            elif nx < 16:
                cn = [lanes(a[nx], j0 + t) for t in range(4)]
            else:
                cn = None
            rp = []
            l = {}
            for t in range(4):
                rp.append(1.0 / s[t, t])
                for i in range(t + 1, 4):
                    l[i, t] = s[i, t] * rp[t]
                for i in range(t + 1, 4):
                    for c in range(t + 1, i + 1):
                        if c == t + 1 and i == c:
                            s[i, c] = s[i, c] - (s[i, t] * s[i, t]) * rp[t]
                        else:
                            s[i, c] = s[i, c] - l[i, t] * s[c, t]
                    rb[i] = rb[i] - l[i, t] * rb[t]
                    if cn is not None:
                        cn[i] = cn[i] - l[i, t] * cn[t]
            if cn is not None:
                base = jnp.where(pivot_lanes, 0.0, a[nx])
                if h == 0:
                    base = jnp.where(sub >= 4, base, a[nx])
                part = [(cn[t] * rp[t]) * rb[t] for t in range(4)]
                a[nx] = ((base - part[0]) - (part[1] + part[2])) - part[3]
            for t in range(4):
                pivots = jnp.where(lane == j0 + t, s[t, t], pivots)
                w = jnp.where(lane < j0 + 4, rb[t] * lax.rsqrt(s[t, t]), 0.0)
                w_out = jnp.where(sub == 4 * h + t, w, w_out)
            x = [None] * 4
            for t in (3, 2, 1, 0):
                x[t] = rb[t] * rp[t]
                for i in range(t + 1, 4):
                    x[t] = x[t] - l[i, t] * x[i]
            for i in range(nx + 1, 16):
                c = [lanes(a[i], j0 + t) for t in range(4)]
                a[i] = jnp.where(pivot_lanes, 0.0, a[i]) - (
                    (c[0] * x[0] + c[1] * x[1]) + (c[2] * x[2] + c[3] * x[3]))
        store(b, w_out)
    return pivots


def main_kernel(ls_ref, ng_ref, co_ref, ob_ref, t_ref, c_ref,
                slab_ref, white_ref, ll_ref,
                a_ref, w_ref, wt_ref, yh_ref, yl_ref, yb_ref, z_ref, m_ref,
                rx_ref, ry_ref, mc_ref, wv_ref, ld_ref, flat_ref):
    prow = lax.axis_index("prow")
    pcol = lax.axis_index("pcol")
    rate = SQRT_THREE / jnp.full((1, 128), ls_ref[0], F32)
    nugget = ng_ref[0]
    lane = lax.broadcasted_iota(jnp.int32, (8, 128), 1)
    sub = lax.broadcasted_iota(jnp.int32, (8, 128), 0)
    rate_t = jnp.concatenate([rate] * 8, 1)
    tx = t_ref[0:1, :] * rate_t
    ty = t_ref[1:2, :] * rate_t
    cx = c_ref[0:1, :] * rate
    cy = c_ref[1:2, :] * rate
    ux = [tx[:, 128 * i:128 * i + 128] for i in range(8)] + [cx]
    uy = [ty[:, 128 * i:128 * i + 128] for i in range(8)] + [cy]

    for q in range(TILES):
        for i in range(4):
            part = slice(128 * i, 128 * i + 128)
            at = slice(q * B + 128 * i, q * B + 128 * i + 128)
            rx_ref[at, :] = jnp.broadcast_to(co_ref[0, q:q + 1, part] * rate, (128, 128)).T
            ry_ref[at, :] = jnp.broadcast_to(co_ref[1, q:q + 1, part] * rate, (128, 128)).T
            flat_ref[4 * q + i:4 * q + i + 1, :] = ob_ref[q:q + 1, part]

    for k in range(NK):
        part = slice(128 * k, 128 * k + 128)
        px = jnp.broadcast_to(tx[:, part], (128, 128)).T
        py = jnp.broadcast_to(ty[:, part], (128, 128)).T
        w_ref[0] = px
        w_ref[1] = py
        wide = lax.broadcasted_iota(jnp.int32, (128, 128), 1)
        a_ref[k, :, T + NC:] = jnp.where(
            wide == 0, jnp.broadcast_to(t_ref[2:3, part], (128, 128)).T, 0.0)

        def build(g, carry, k=k):
            at = pl.ds(pl.multiple_of(8 * g, 8), 8)
            gx = w_ref[0, at, :]
            gy = w_ref[1, at, :]
            for j in range(k, 9):
                v = matern(gx - ux[j], gy - uy[j])
                if j == k:
                    v = v + jnp.where(lane == sub + 8 * g, nugget, 0.0)
                a_ref[k, at, 128 * j:128 * j + 128] = v
            return carry
        lax.fori_loop(0, 16, build, 0)

    ld_ref[...] = jnp.zeros((8, 128), F32)

    def step(k, carry):
        off = pl.ds(pl.multiple_of(128 * k, 128), 128)

        def load(i):
            return a_ref[k, 8 * i:8 * i + 8, off]

        def store(i, w):
            w_ref[k, 8 * i:8 * i + 8, :] = w

        pivots = factor_block(load, store)
        ld_ref[...] = ld_ref[...] + jnp.log(pivots)
        for kk in range(NK):
            @pl.when(k == kk)
            def _():
                o = 128 * (kk + 1)
                n = WIDTH - o
                w = w_ref[kk]
                wt_ref[kk] = w.T
                y = mm3(w, a_ref[kk, :, o:])
                yh, yl = split(y)
                if kk < NK - 1:
                    yh_ref[kk, :, o:T] = yh[:, :n - 256]
                    yl_ref[kk, :, o:T] = yl[:, :n - 256]
                yb_ref[kk] = y[:, n - 256:]
                z_ref[kk:kk + 1, :] = y[:, n - 128:].T[0:1, :]
                ycat = jnp.concatenate([yh, yl, yh], 0)
                for i in range(kk + 1, NK):
                    f = 128 * (i - kk - 1)
                    th, tl = split(y[:, f:f + 128].T)
                    tcat = jnp.concatenate([th, th, tl], 1)
                    a_ref[i, :, 128 * i:] = a_ref[i, :, 128 * i:] - mm(tcat, ycat[:, f:])
        return carry
    lax.fori_loop(0, NK, step, 0)

    for k in range(NK - 1, -1, -1):
        acc = yb_ref[k]
        if k < NK - 1:
            o = 128 * (k + 1)
            mh, ml = split(m_ref[o:, :])
            yh = yh_ref[k, :, o:T]
            acc = acc - (mm(yh, mh) + mm(yh, ml) + mm(yl_ref[k, :, o:T], mh))
        m_ref[128 * k:128 * k + 128, :] = mm3(wt_ref[k], acc)

    mh, ml = split(m_ref[:, :NC])
    mc_ref[:, :NC] = mh
    mc_ref[:, NC:] = ml
    wt = m_ref[:, NC:].T
    wh, wl = split(wt[0:1, :])
    wv_ref[...] = jnp.concatenate([wh, wl, jnp.zeros((14, T), BF16)], 0)

    z = z_ref[...]
    total = jnp.sum(z * z) + jnp.sum(ld_ref[0:1, :])
    ll_ref[...] = jnp.full((1, 128), total * (-0.5 / T), F32)

    wl_ = lax.broadcasted_iota(jnp.int32, (128, 128), 1)
    ws_ = lax.broadcasted_iota(jnp.int32, (128, 128), 0)

    def body(q, carry):
        panel = (q == 0) & (prow < 2)
        for j in range(4):
            at = pl.ds(pl.multiple_of(512 * q + 128 * j, 128), 128)
            gx = rx_ref[at, :]
            gy = ry_ref[at, :]
            acc = None
            for t in range(4):
                piece = jnp.concatenate(
                    [matern(gx - ux[2 * t + e], gy - uy[2 * t + e]) for e in range(2)], 1)
                ch, cl = split(piece)
                mt = mc_ref[256 * t:256 * t + 256, :]
                wv = wv_ref[:, 256 * t:256 * t + 256]
                both = mm(ch, mt)
                low = mm(cl, mt[:, :NC])
                wr = lax.dot_general(wv, ch, (((1,), (1,)), ((), ())), preferred_element_type=F32)
                wr2 = lax.dot_general(wv, cl, (((1,), (1,)), ((), ())), preferred_element_type=F32)
                cur = (both[:, :NC] + both[:, NC:] + low, wr[0:1] + wr[1:2] + wr2[0:1])
                acc = cur if acc is None else (acc[0] + cur[0], acc[1] + cur[1])
            first = (q * N_PROW + prow) * B + 128 * j - (T + pcol * NC)
            value = matern(gx - cx, gy - cy) + jnp.where(wl_ == ws_ + first, nugget, 0.0) - acc[0]
            slab_ref[q, 128 * j:128 * j + 128, :] = jnp.where(panel, 0.0, value)
            zr = z_ref[pl.ds(jnp.minimum(prow, 1) * 4 + j, 1), :]
            flat_ref[pl.ds(4 * q + j, 1), :] = jnp.where(panel, zr, flat_ref[pl.ds(4 * q + j, 1), :] - acc[1])
        return carry
    lax.fori_loop(0, TILES, body, 0)
    for r in range(32):
        white_ref[r // 4:r // 4 + 1, 128 * (r % 4):128 * (r % 4) + 128] = flat_ref[r:r + 1, :]


def main_call(length_scale, nugget, coords, observations, sites, columns):
    vm = pl.BlockSpec(memory_space=pltpu.VMEM)
    sm = pl.BlockSpec(memory_space=pltpu.SMEM)
    return pl.pallas_call(
        main_kernel,
        out_shape=(jax.ShapeDtypeStruct((TILES, B, NC), F32),
                   jax.ShapeDtypeStruct((TILES, B), F32),
                   jax.ShapeDtypeStruct((1, 128), F32)),
        in_specs=[sm, sm, vm, vm, vm, vm], out_specs=(vm, vm, vm),
        scratch_shapes=[
            pltpu.VMEM((NK, NB, WIDTH), F32),
            pltpu.VMEM((NK, NB, NB), F32),
            pltpu.VMEM((NK, NB, NB), F32),
            pltpu.VMEM((NK, NB, T), BF16),
            pltpu.VMEM((NK, NB, T), BF16),
            pltpu.VMEM((NK, NB, 2 * NC), F32),
            pltpu.VMEM((NK, NB), F32),
            pltpu.VMEM((T, 2 * NC), F32),
            pltpu.VMEM((TILES * B, 128), F32),
            pltpu.VMEM((TILES * B, 128), F32),
            pltpu.VMEM((T, 2 * NC), BF16),
            pltpu.VMEM((16, T), BF16),
            pltpu.VMEM((8, 128), F32),
            pltpu.VMEM((32, 128), F32),
        ],
        compiler_params=pltpu.CompilerParams(vmem_limit_bytes=60 * 1024 * 1024),
        name="factor_and_slab",
    )(length_scale, nugget, coords, observations, sites, columns)


def shards(coords, observations, length_scale, nugget):
    pk = jnp.concatenate([coords[:, 0, :], observations[0:1], observations[0:1]], 0)
    sites, columns = gather_sites(pk)
    slab, white, ll = main_call(length_scale, nugget, coords, observations, sites, columns)
    return slab, white, ll[0, :1]


def solution(mesh):
    placed = (P(None, None, "prow"), P(None, "prow"), P(), P())
    return jax.shard_map(
        shards,
        mesh=mesh,
        in_specs=placed,
        out_specs=(P(None, "prow", "pcol"), P(None, "prow"), P()),
        check_vma=False,
    )
```

```python
import math

import jax
import jax.numpy as jnp
from jax import lax
from jax.experimental import pallas as pl
from jax.experimental.pallas import tpu as pltpu
from jax.sharding import PartitionSpec as P

SQRT_THREE = math.sqrt(3.0)
MINUS_LOG2E = -math.log2(math.e)
F32 = jnp.float32
BF16 = jnp.bfloat16
MESH = pl.DeviceIdType.MESH

B = 512
T = 2 * B
NB = 128
SP = 64
PW = 16
NK = T // NB
N_PROW = 16
TILES = 8
NC = 128
WIDTH = T + 2 * NC


def gather_kernel(pk_ref, t_ref, c_ref, t0, t1, tc, send_sem, recv_sem):
    prow = lax.axis_index("prow")
    pcol = lax.axis_index("pcol")
    col_owner = 2 + pcol // 4
    part = pl.ds(pl.multiple_of((pcol % 4) * NC, NC), NC)
    barrier = pltpu.get_barrier_semaphore()
    senders = ((0, 0), (1, 1), (col_owner, 2))
    for owner, _ in senders:
        @pl.when(prow != owner)
        def _():
            pl.semaphore_signal(barrier, inc=1, device_id=(owner, pcol), device_id_type=MESH)

    sources = (pk_ref, pk_ref, pk_ref.at[:, part])
    slots = (t0, t1, tc)

    def copy(slot, step, target):
        return pltpu.make_async_remote_copy(
            src_ref=sources[slot], dst_ref=slots[slot],
            send_sem=send_sem.at[step], recv_sem=recv_sem.at[slot],
            device_id=(target, pcol), device_id_type=MESH)

    for owner, slot in senders:
        @pl.when(prow == owner)
        def _():
            pl.semaphore_wait(barrier, N_PROW - 1)
            for step in range(1, N_PROW):
                copy(slot, step, (prow + step) % N_PROW).start()
            slots[slot][...] = sources[slot][...]
            for step in range(1, N_PROW):
                copy(slot, step, (prow + step) % N_PROW).wait_send()
    for owner, slot in senders:
        @pl.when(prow != owner)
        def _():
            copy(slot, 1, (prow + 1) % N_PROW).wait_recv()
    t_ref[:, :B] = t0[...]
    t_ref[:, B:] = t1[...]
    c_ref[...] = tc[...]


def gather_sites(pk):
    vm = pl.BlockSpec(memory_space=pltpu.VMEM)
    return pl.pallas_call(
        gather_kernel,
        out_shape=(jax.ShapeDtypeStruct((4, T), F32), jax.ShapeDtypeStruct((4, NC), F32)),
        in_specs=[vm], out_specs=(vm, vm),
        scratch_shapes=[
            pltpu.VMEM((4, B), F32), pltpu.VMEM((4, B), F32), pltpu.VMEM((4, NC), F32),
            pltpu.SemaphoreType.DMA((N_PROW,)), pltpu.SemaphoreType.DMA((3,)),
        ],
        compiler_params=pltpu.CompilerParams(collective_id=0, has_side_effects=True),
        name="gather_sites",
    )(pk)


def split(x):
    high = x.astype(BF16)
    return high, (x - high.astype(F32)).astype(BF16)


def matern(dx, dy):
    s = 1.0 / lax.rsqrt(dx * dx + dy * dy)
    return (1.0 + s) * jnp.exp2(s * MINUS_LOG2E)


def lanes(x, j):
    return jnp.broadcast_to(x[:, j:j + 1], (8, 128))


def rows(x, i):
    return jnp.take_along_axis(x, jnp.full((8, 128), i, jnp.int32), axis=0)


def mm(x, y):
    return lax.dot_general(x, y, (((1,), (0,)), ((), ())), preferred_element_type=F32)


def mm3(x, y):
    xh, xl = split(x)
    yh, yl = split(y)
    return mm(jnp.concatenate([xh, xh, xl], 1), jnp.concatenate([yh, yl, yh], 0))


def factor_block(d_ref, w_ref, k):
    lane = lax.broadcasted_iota(jnp.int32, (8, 128), 1)
    sub = lax.broadcasted_iota(jnp.int32, (8, 128), 0)
    wide = lax.broadcasted_iota(jnp.int32, (SP, 128), 1)
    nv = SP // 8
    logs = jnp.zeros((8, 128), F32)
    for p in range(NB // SP):
        r0 = SP * p
        a = [d_ref[r0 + 8 * i:r0 + 8 * i + 8, :] for i in range(nv)]
        d = [jnp.ones((8, 128), F32) for _ in range(nv)]
        for c0 in range(0, SP, PW):
            own = range(c0 // 8, (c0 + PW) // 8)
            cols = {(t, v): lanes(a[v], r0 + t)
                    for t in range(c0, c0 + PW) for v in range(t // 8, nv)}
            group = (lane >= r0 + c0) & (lane < r0 + c0 + PW)
            for v in range(c0 // 8, nv):
                fill = jnp.where((lane - r0) == (sub + 8 * v), 1.0, 0.0) if v in own else 0.0
                a[v] = jnp.where(group, fill, a[v])
            for t in range(c0, c0 + PW):
                vt, st = t // 8, t % 8
                pivot = rows(cols[t, vt], st)
                d[vt] = jnp.where(sub == st, pivot, d[vt])
                rp = 1.0 / pivot
                m = {v: cols[t, v] * rp for v in range(vt, nv)}
                for i in range(t + 1, c0 + PW):
                    entry = rows(cols[t, i // 8], i % 8)
                    for v in range(i // 8, nv):
                        if i == t + 1 and v == i // 8:
                            cols[i, v] = cols[i, v] - (cols[t, v] * entry) * rp
                        else:
                            cols[i, v] = cols[i, v] - m[v] * entry
                row = rows(a[vt], st)
                for v in range(vt, nv):
                    mv = jnp.where(sub > st, m[v], 0.0) if v == vt else m[v]
                    a[v] = a[v] - mv * row
        y_out = []
        for v in range(nv):
            y = a[v] * lax.rsqrt(d[v])
            logs = logs + jnp.log(d[v])
            y_out.append(jnp.where((lane > r0 + 8 * v + sub) & (lane < r0 + SP), 0.0, y))
        y = jnp.concatenate(y_out, 0)
        w_ref[k, r0:r0 + SP, :] = jnp.where(wide < r0 + SP, y, 0.0)
        if r0 + SP < NB:
            yh, yl = split(y)
            left = jnp.concatenate([yh.astype(F32), yh.astype(F32), yl.astype(F32)], 0).T
            left = left[r0 + SP:, :].astype(BF16)
            update = mm(left, jnp.concatenate([yh, yl, yh], 0))
            rest = d_ref[r0 + SP:, :]
            own = lax.broadcasted_iota(jnp.int32, rest.shape, 1)
            own = (own >= r0) & (own < r0 + SP)
            d_ref[r0 + SP:, :] = jnp.where(own, 0.0, rest) - update
    return logs


def main_kernel(ls_ref, ng_ref, co_ref, ob_ref, t_ref, c_ref,
                slab_ref, white_ref, ll_ref,
                a_ref, w_ref, wt_ref, yh_ref, yl_ref, yb_ref, z_ref, m_ref,
                rx_ref, ry_ref, mc_ref, wv_ref, ld_ref, flat_ref, d_ref):
    prow = lax.axis_index("prow")
    pcol = lax.axis_index("pcol")
    rate = SQRT_THREE / jnp.full((1, 128), ls_ref[0], F32)
    nugget = ng_ref[0]
    lane = lax.broadcasted_iota(jnp.int32, (8, 128), 1)
    sub = lax.broadcasted_iota(jnp.int32, (8, 128), 0)
    rate_t = jnp.concatenate([rate] * 8, 1)
    tx = t_ref[0:1, :] * rate_t
    ty = t_ref[1:2, :] * rate_t
    cx = c_ref[0:1, :] * rate
    cy = c_ref[1:2, :] * rate
    ux = [tx[:, 128 * i:128 * i + 128] for i in range(8)] + [cx]
    uy = [ty[:, 128 * i:128 * i + 128] for i in range(8)] + [cy]

    for q in range(TILES):
        for i in range(4):
            part = slice(128 * i, 128 * i + 128)
            at = slice(q * B + 128 * i, q * B + 128 * i + 128)
            rx_ref[at, :] = jnp.broadcast_to(co_ref[0, q:q + 1, part] * rate, (128, 128)).T
            ry_ref[at, :] = jnp.broadcast_to(co_ref[1, q:q + 1, part] * rate, (128, 128)).T
            flat_ref[4 * q + i:4 * q + i + 1, :] = ob_ref[q:q + 1, part]

    for k in range(NK):
        part = slice(128 * k, 128 * k + 128)
        px = jnp.broadcast_to(tx[:, part], (128, 128)).T
        py = jnp.broadcast_to(ty[:, part], (128, 128)).T
        w_ref[0] = px
        w_ref[1] = py
        wide = lax.broadcasted_iota(jnp.int32, (128, 128), 1)
        a_ref[k, :, T + NC:] = jnp.where(
            wide == 0, jnp.broadcast_to(t_ref[2:3, part], (128, 128)).T, 0.0)

        def build(g, carry, k=k):
            at = pl.ds(pl.multiple_of(8 * g, 8), 8)
            gx = w_ref[0, at, :]
            gy = w_ref[1, at, :]
            for j in range(k, 9):
                v = matern(gx - ux[j], gy - uy[j])
                if j == k:
                    v = v + jnp.where(lane == sub + 8 * g, nugget, 0.0)
                a_ref[k, at, 128 * j:128 * j + 128] = v
            return carry
        lax.fori_loop(0, 16, build, 0)

    ld_ref[...] = jnp.zeros((8, 128), F32)

    def step(k, carry):
        off = pl.ds(pl.multiple_of(128 * k, 128), 128)

        d_ref[...] = a_ref[k, :, off]
        ld_ref[...] = ld_ref[...] + factor_block(d_ref, w_ref, k)
        for kk in range(NK):
            @pl.when(k == kk)
            def _():
                o = 128 * (kk + 1)
                n = WIDTH - o
                w = w_ref[kk]
                wt_ref[kk] = w.T
                y = mm3(w, a_ref[kk, :, o:])
                yh, yl = split(y)
                if kk < NK - 1:
                    yh_ref[kk, :, o:T] = yh[:, :n - 256]
                    yl_ref[kk, :, o:T] = yl[:, :n - 256]
                yb_ref[kk] = y[:, n - 256:]
                z_ref[kk:kk + 1, :] = y[:, n - 128:].T[0:1, :]
                ycat = jnp.concatenate([yh, yl, yh], 0)
                for i in range(kk + 1, NK):
                    f = 128 * (i - kk - 1)
                    th, tl = split(y[:, f:f + 128].T)
                    tcat = jnp.concatenate([th, th, tl], 1)
                    a_ref[i, :, 128 * i:] = a_ref[i, :, 128 * i:] - mm(tcat, ycat[:, f:])
        return carry
    lax.fori_loop(0, NK, step, 0)

    for k in range(NK - 1, -1, -1):
        acc = yb_ref[k]
        if k < NK - 1:
            o = 128 * (k + 1)
            mh, ml = split(m_ref[o:, :])
            yh = yh_ref[k, :, o:T]
            acc = acc - (mm(yh, mh) + mm(yh, ml) + mm(yl_ref[k, :, o:T], mh))
        m_ref[128 * k:128 * k + 128, :] = mm3(wt_ref[k], acc)

    mh, ml = split(m_ref[:, :NC])
    mc_ref[:, :NC] = mh
    mc_ref[:, NC:] = ml
    wt = m_ref[:, NC:].T
    wh, wl = split(wt[0:1, :])
    wv_ref[...] = jnp.concatenate([wh, wl, jnp.zeros((14, T), BF16)], 0)

    z = z_ref[...]
    total = jnp.sum(z * z) + jnp.sum(ld_ref[:, 0:1])
    ll_ref[...] = jnp.full((1, 128), total * (-0.5 / T), F32)

    wl_ = lax.broadcasted_iota(jnp.int32, (128, 128), 1)
    ws_ = lax.broadcasted_iota(jnp.int32, (128, 128), 0)

    def body(q, carry):
        panel = (q == 0) & (prow < 2)
        for j in range(4):
            at = pl.ds(pl.multiple_of(512 * q + 128 * j, 128), 128)
            gx = rx_ref[at, :]
            gy = ry_ref[at, :]
            acc = None
            for t in range(4):
                piece = jnp.concatenate(
                    [matern(gx - ux[2 * t + e], gy - uy[2 * t + e]) for e in range(2)], 1)
                ch, cl = split(piece)
                mt = mc_ref[256 * t:256 * t + 256, :]
                wv = wv_ref[:, 256 * t:256 * t + 256]
                both = mm(ch, mt)
                low = mm(cl, mt[:, :NC])
                wr = lax.dot_general(wv, ch, (((1,), (1,)), ((), ())), preferred_element_type=F32)
                wr2 = lax.dot_general(wv, cl, (((1,), (1,)), ((), ())), preferred_element_type=F32)
                cur = (both[:, :NC] + both[:, NC:] + low, wr[0:1] + wr[1:2] + wr2[0:1])
                acc = cur if acc is None else (acc[0] + cur[0], acc[1] + cur[1])
            first = (q * N_PROW + prow) * B + 128 * j - (T + pcol * NC)
            value = matern(gx - cx, gy - cy) + jnp.where(wl_ == ws_ + first, nugget, 0.0) - acc[0]
            slab_ref[q, 128 * j:128 * j + 128, :] = jnp.where(panel, 0.0, value)
            zr = z_ref[pl.ds(jnp.minimum(prow, 1) * 4 + j, 1), :]
            flat_ref[pl.ds(4 * q + j, 1), :] = jnp.where(panel, zr, flat_ref[pl.ds(4 * q + j, 1), :] - acc[1])
        return carry
    lax.fori_loop(0, TILES, body, 0)
    for r in range(32):
        white_ref[r // 4:r // 4 + 1, 128 * (r % 4):128 * (r % 4) + 128] = flat_ref[r:r + 1, :]


def main_call(length_scale, nugget, coords, observations, sites, columns):
    vm = pl.BlockSpec(memory_space=pltpu.VMEM)
    sm = pl.BlockSpec(memory_space=pltpu.SMEM)
    return pl.pallas_call(
        main_kernel,
        out_shape=(jax.ShapeDtypeStruct((TILES, B, NC), F32),
                   jax.ShapeDtypeStruct((TILES, B), F32),
                   jax.ShapeDtypeStruct((1, 128), F32)),
        in_specs=[sm, sm, vm, vm, vm, vm], out_specs=(vm, vm, vm),
        scratch_shapes=[
            pltpu.VMEM((NK, NB, WIDTH), F32),
            pltpu.VMEM((NK, NB, NB), F32),
            pltpu.VMEM((NK, NB, NB), F32),
            pltpu.VMEM((NK, NB, T), BF16),
            pltpu.VMEM((NK, NB, T), BF16),
            pltpu.VMEM((NK, NB, 2 * NC), F32),
            pltpu.VMEM((NK, NB), F32),
            pltpu.VMEM((T, 2 * NC), F32),
            pltpu.VMEM((TILES * B, 128), F32),
            pltpu.VMEM((TILES * B, 128), F32),
            pltpu.VMEM((T, 2 * NC), BF16),
            pltpu.VMEM((16, T), BF16),
            pltpu.VMEM((8, 128), F32),
            pltpu.VMEM((32, 128), F32),
            pltpu.VMEM((NB, NB), F32),
        ],
        compiler_params=pltpu.CompilerParams(vmem_limit_bytes=60 * 1024 * 1024),
        name="factor_and_slab",
    )(length_scale, nugget, coords, observations, sites, columns)


def shards(coords, observations, length_scale, nugget):
    pk = jnp.concatenate([coords[:, 0, :], observations[0:1], observations[0:1]], 0)
    sites, columns = gather_sites(pk)
    slab, white, ll = main_call(length_scale, nugget, coords, observations, sites, columns)
    return slab, white, ll[0, :1]


def solution(mesh):
    placed = (P(None, None, "prow"), P(None, "prow"), P(), P())
    return jax.shard_map(
        shards,
        mesh=mesh,
        in_specs=placed,
        out_specs=(P(None, "prow", "pcol"), P(None, "prow"), P()),
        check_vma=False,
    )
```

```python
import math

import jax
import jax.numpy as jnp
from jax import lax
from jax.experimental import pallas as pl
from jax.experimental.pallas import tpu as pltpu
from jax.sharding import PartitionSpec as P

SQRT_THREE = math.sqrt(3.0)
MINUS_LOG2E = -math.log2(math.e)
F32 = jnp.float32
BF16 = jnp.bfloat16
MESH = pl.DeviceIdType.MESH

B = 512
T = 2 * B
NB = 128
SP = 64
PW = 16
NK = T // NB
N_PROW = 16
HALF = 8
TILES = 8
NC = 128
WIDTH = T + 2 * NC


def gather_kernel(co_ref, ob_ref, t_ref, c_ref, xy0, xy1, xyc, ob0, ob1,
                  send_sem, relay_sem, recv_sem, own_sem):
    prow = lax.axis_index("prow")
    pcol = lax.axis_index("pcol")
    half = prow // HALF
    local = prow % HALF
    line = (pcol // 4) * 4
    zlo = pcol % 4
    near = line + jnp.where(zlo < 2, 3, 0)
    feeds = jnp.where(zlo == 3, 0, 2)
    feeder = (half == 0) & ((zlo == 0) | (zlo == 3))
    owners = (0, 1, 2 + pcol // 4)

    def part(z):
        return pl.ds(pl.multiple_of(z * NC, NC), NC)

    def pieces(slot, z):
        if slot == 2:
            return ((co_ref.at[:, 0:1, part(z)], xyc.at[:, 0:1, :]),)
        xy, ob = ((xy0, ob0), (xy1, ob1))[slot]
        return ((co_ref.at[:, 0:1, :], xy.at[:, 0:1, :]), (ob_ref.at[0:1, :], ob.at[0:1, :]))

    barrier = pltpu.get_barrier_semaphore()
    for slot, owner in enumerate(owners):
        @pl.when(local != owner)
        def _():
            pl.semaphore_signal(barrier, inc=1, device_id=(half * HALF + owner, pcol),
                                device_id_type=MESH)

        @pl.when((local == owner) & (half == 1))
        def _():
            pl.semaphore_signal(barrier, inc=1, device_id=(owner, near), device_id_type=MESH)

    def remote(slot, piece, src, dst, sem, target):
        return pltpu.make_async_remote_copy(
            src_ref=src, dst_ref=dst, send_sem=sem, recv_sem=recv_sem.at[slot, piece],
            device_id=target, device_id_type=MESH)

    def spread(slot, owner, from_slot):
        out = []
        for step in range(1, HALF):
            target = (half * HALF + (local + step) % HALF, pcol)
            for n, (src, dst) in enumerate(pieces(slot, zlo)):
                out.append(remote(slot, n, dst if from_slot else src, dst,
                                  send_sem.at[step, n], target))
        return out

    def feed(slot):
        out = []
        for e in range(2):
            target = (prow + HALF, line + feeds + e)
            for n, (src, dst) in enumerate(pieces(slot, feeds + e)):
                out.append(remote(slot, n, src, dst, relay_sem.at[e, n], target))
        return out

    for slot, owner in enumerate(owners):
        @pl.when((local == owner) & (half == 0))
        def _():
            @pl.when(feeder)
            def _():
                pl.semaphore_wait(barrier, HALF + 1)
                for c in feed(slot):
                    c.start()

            @pl.when(jnp.logical_not(feeder))
            def _():
                pl.semaphore_wait(barrier, HALF - 1)
            for c in spread(slot, owner, False):
                c.start()
            mine = [pltpu.make_async_copy(src, dst, own_sem.at[n])
                    for n, (src, dst) in enumerate(pieces(slot, zlo))]
            for c in mine:
                c.start()
            for c in mine:
                c.wait()
            for c in spread(slot, owner, False):
                c.wait_send()

            @pl.when(feeder)
            def _():
                for c in feed(slot):
                    c.wait_send()

        @pl.when((local == owner) & (half == 1))
        def _():
            pl.semaphore_wait(barrier, HALF - 1)
            copies = spread(slot, owner, True)
            for c in copies[:len(pieces(slot, zlo))]:
                c.wait_recv()
            for c in copies:
                c.start()
            for c in copies:
                c.wait_send()

    for slot, owner in enumerate(owners):
        @pl.when(local != owner)
        def _():
            for c in spread(slot, owner, False)[:len(pieces(slot, zlo))]:
                c.wait_recv()
    for slot, (xy, ob) in enumerate(((xy0, ob0), (xy1, ob1))):
        at = slice(slot * B, slot * B + B)
        t_ref[0:1, at] = xy[0, 0:1, :]
        t_ref[1:2, at] = xy[1, 0:1, :]
        t_ref[2:3, at] = ob[0:1, :]
    c_ref[0:1, :] = xyc[0, 0:1, :]
    c_ref[1:2, :] = xyc[1, 0:1, :]


def gather_sites(coords, observations):
    vm = pl.BlockSpec(memory_space=pltpu.VMEM)
    stay = pl.BlockSpec(memory_space=pl.ANY)
    return pl.pallas_call(
        gather_kernel,
        out_shape=(jax.ShapeDtypeStruct((4, T), F32), jax.ShapeDtypeStruct((4, NC), F32)),
        in_specs=[stay, stay], out_specs=(vm, vm),
        scratch_shapes=[
            pltpu.VMEM((2, 8, B), F32), pltpu.VMEM((2, 8, B), F32), pltpu.VMEM((2, 8, NC), F32),
            pltpu.VMEM((8, B), F32), pltpu.VMEM((8, B), F32),
            pltpu.SemaphoreType.DMA((HALF, 2)), pltpu.SemaphoreType.DMA((2, 2)),
            pltpu.SemaphoreType.DMA((3, 2)), pltpu.SemaphoreType.DMA((2,)),
        ],
        compiler_params=pltpu.CompilerParams(collective_id=0, has_side_effects=True),
        name="gather_sites",
    )(coords, observations)


def split(x):
    high = x.astype(BF16)
    return high, (x - high.astype(F32)).astype(BF16)


def matern(dx, dy):
    s = 1.0 / lax.rsqrt(dx * dx + dy * dy)
    return (1.0 + s) * jnp.exp2(s * MINUS_LOG2E)


def lanes(x, j):
    return jnp.broadcast_to(x[:, j:j + 1], (8, 128))


def rows(x, i):
    return jnp.take_along_axis(x, jnp.full((8, 128), i, jnp.int32), axis=0)


def mm(x, y):
    return lax.dot_general(x, y, (((1,), (0,)), ((), ())), preferred_element_type=F32)


def mm3(x, y):
    xh, xl = split(x)
    yh, yl = split(y)
    return mm(jnp.concatenate([xh, xh, xl], 1), jnp.concatenate([yh, yl, yh], 0))


def factor_block(d_ref, w_ref, k):
    lane = lax.broadcasted_iota(jnp.int32, (8, 128), 1)
    sub = lax.broadcasted_iota(jnp.int32, (8, 128), 0)
    wide = lax.broadcasted_iota(jnp.int32, (SP, 128), 1)
    nv = SP // 8
    logs = jnp.zeros((8, 128), F32)
    for p in range(NB // SP):
        r0 = SP * p
        a = [d_ref[r0 + 8 * i:r0 + 8 * i + 8, :] for i in range(nv)]
        d = [jnp.ones((8, 128), F32) for _ in range(nv)]
        for c0 in range(0, SP, PW):
            own = range(c0 // 8, (c0 + PW) // 8)
            cols = {(t, v): lanes(a[v], r0 + t)
                    for t in range(c0, c0 + PW) for v in range(t // 8, nv)}
            group = (lane >= r0 + c0) & (lane < r0 + c0 + PW)
            for v in range(c0 // 8, nv):
                fill = jnp.where((lane - r0) == (sub + 8 * v), 1.0, 0.0) if v in own else 0.0
                a[v] = jnp.where(group, fill, a[v])
            for t in range(c0, c0 + PW):
                vt, st = t // 8, t % 8
                pivot = rows(cols[t, vt], st)
                d[vt] = jnp.where(sub == st, pivot, d[vt])
                rp = 1.0 / pivot
                m = {v: cols[t, v] * rp for v in range(vt, nv)}
                for i in range(t + 1, c0 + PW):
                    entry = rows(cols[t, i // 8], i % 8)
                    for v in range(i // 8, nv):
                        if i == t + 1 and v == i // 8:
                            cols[i, v] = cols[i, v] - (cols[t, v] * entry) * rp
                        else:
                            cols[i, v] = cols[i, v] - m[v] * entry
                row = rows(a[vt], st)
                for v in range(vt, nv):
                    mv = jnp.where(sub > st, m[v], 0.0) if v == vt else m[v]
                    a[v] = a[v] - mv * row
        y_out = []
        for v in range(nv):
            y = a[v] * lax.rsqrt(d[v])
            logs = logs + jnp.log(d[v])
            y_out.append(jnp.where((lane > r0 + 8 * v + sub) & (lane < r0 + SP), 0.0, y))
        y = jnp.concatenate(y_out, 0)
        w_ref[k, r0:r0 + SP, :] = jnp.where(wide < r0 + SP, y, 0.0)
        if r0 + SP < NB:
            yh, yl = split(y)
            left = jnp.concatenate([yh.astype(F32), yh.astype(F32), yl.astype(F32)], 0).T
            left = left[r0 + SP:, :].astype(BF16)
            update = mm(left, jnp.concatenate([yh, yl, yh], 0))
            rest = d_ref[r0 + SP:, :]
            own = lax.broadcasted_iota(jnp.int32, rest.shape, 1)
            own = (own >= r0) & (own < r0 + SP)
            d_ref[r0 + SP:, :] = jnp.where(own, 0.0, rest) - update
    return logs


def main_kernel(ls_ref, ng_ref, co_ref, ob_ref, t_ref, c_ref,
                slab_ref, white_ref, ll_ref,
                a_ref, w_ref, wt_ref, yh_ref, yl_ref, yb_ref, z_ref, m_ref,
                rx_ref, ry_ref, mc_ref, wv_ref, ld_ref, flat_ref, d_ref):
    prow = lax.axis_index("prow")
    pcol = lax.axis_index("pcol")
    rate = SQRT_THREE / jnp.full((1, 128), ls_ref[0], F32)
    nugget = ng_ref[0]
    lane = lax.broadcasted_iota(jnp.int32, (8, 128), 1)
    sub = lax.broadcasted_iota(jnp.int32, (8, 128), 0)
    rate_t = jnp.concatenate([rate] * 8, 1)
    tx = t_ref[0:1, :] * rate_t
    ty = t_ref[1:2, :] * rate_t
    cx = c_ref[0:1, :] * rate
    cy = c_ref[1:2, :] * rate
    ux = [tx[:, 128 * i:128 * i + 128] for i in range(8)] + [cx]
    uy = [ty[:, 128 * i:128 * i + 128] for i in range(8)] + [cy]

    for q in range(TILES):
        for i in range(4):
            part = slice(128 * i, 128 * i + 128)
            at = slice(q * B + 128 * i, q * B + 128 * i + 128)
            rx_ref[at, :] = jnp.broadcast_to(co_ref[0, q:q + 1, part] * rate, (128, 128)).T
            ry_ref[at, :] = jnp.broadcast_to(co_ref[1, q:q + 1, part] * rate, (128, 128)).T
            flat_ref[4 * q + i:4 * q + i + 1, :] = ob_ref[q:q + 1, part]

    for k in range(NK):
        part = slice(128 * k, 128 * k + 128)
        px = jnp.broadcast_to(tx[:, part], (128, 128)).T
        py = jnp.broadcast_to(ty[:, part], (128, 128)).T
        w_ref[0] = px
        w_ref[1] = py
        wide = lax.broadcasted_iota(jnp.int32, (128, 128), 1)
        a_ref[k, :, T + NC:] = jnp.where(
            wide == 0, jnp.broadcast_to(t_ref[2:3, part], (128, 128)).T, 0.0)

        def build(g, carry, k=k):
            at = pl.ds(pl.multiple_of(8 * g, 8), 8)
            gx = w_ref[0, at, :]
            gy = w_ref[1, at, :]
            for j in range(k, 9):
                v = matern(gx - ux[j], gy - uy[j])
                if j == k:
                    v = v + jnp.where(lane == sub + 8 * g, nugget, 0.0)
                a_ref[k, at, 128 * j:128 * j + 128] = v
            return carry
        lax.fori_loop(0, 16, build, 0)

    ld_ref[...] = jnp.zeros((8, 128), F32)

    def step(k, carry):
        off = pl.ds(pl.multiple_of(128 * k, 128), 128)

        d_ref[...] = a_ref[k, :, off]
        ld_ref[...] = ld_ref[...] + factor_block(d_ref, w_ref, k)
        for kk in range(NK):
            @pl.when(k == kk)
            def _():
                o = 128 * (kk + 1)
                n = WIDTH - o
                w = w_ref[kk]
                wt_ref[kk] = w.T
                y = mm3(w, a_ref[kk, :, o:])
                yh, yl = split(y)
                if kk < NK - 1:
                    yh_ref[kk, :, o:T] = yh[:, :n - 256]
                    yl_ref[kk, :, o:T] = yl[:, :n - 256]
                yb_ref[kk] = y[:, n - 256:]
                z_ref[kk:kk + 1, :] = y[:, n - 128:].T[0:1, :]
                ycat = jnp.concatenate([yh, yl, yh], 0)
                for i in range(kk + 1, NK):
                    f = 128 * (i - kk - 1)
                    th, tl = split(y[:, f:f + 128].T)
                    tcat = jnp.concatenate([th, th, tl], 1)
                    a_ref[i, :, 128 * i:] = a_ref[i, :, 128 * i:] - mm(tcat, ycat[:, f:])
        return carry
    lax.fori_loop(0, NK, step, 0)

    for k in range(NK - 1, -1, -1):
        acc = yb_ref[k]
        if k < NK - 1:
            o = 128 * (k + 1)
            mh, ml = split(m_ref[o:, :])
            yh = yh_ref[k, :, o:T]
            acc = acc - (mm(yh, mh) + mm(yh, ml) + mm(yl_ref[k, :, o:T], mh))
        m_ref[128 * k:128 * k + 128, :] = mm3(wt_ref[k], acc)

    mh, ml = split(m_ref[:, :NC])
    mc_ref[:, :NC] = mh
    mc_ref[:, NC:] = ml
    wt = m_ref[:, NC:].T
    wh, wl = split(wt[0:1, :])
    wv_ref[...] = jnp.concatenate([wh, wl, jnp.zeros((14, T), BF16)], 0)

    z = z_ref[...]
    total = jnp.sum(z * z) + jnp.sum(ld_ref[:, 0:1])
    ll_ref[...] = jnp.full((1, 128), total * (-0.5 / T), F32)

    wl_ = lax.broadcasted_iota(jnp.int32, (128, 128), 1)
    ws_ = lax.broadcasted_iota(jnp.int32, (128, 128), 0)

    def body(q, carry):
        panel = (q == 0) & (prow < 2)
        for j in range(4):
            at = pl.ds(pl.multiple_of(512 * q + 128 * j, 128), 128)
            gx = rx_ref[at, :]
            gy = ry_ref[at, :]
            acc = None
            for t in range(4):
                piece = jnp.concatenate(
                    [matern(gx - ux[2 * t + e], gy - uy[2 * t + e]) for e in range(2)], 1)
                ch, cl = split(piece)
                mt = mc_ref[256 * t:256 * t + 256, :]
                wv = wv_ref[:, 256 * t:256 * t + 256]
                both = mm(ch, mt)
                low = mm(cl, mt[:, :NC])
                wr = lax.dot_general(wv, ch, (((1,), (1,)), ((), ())), preferred_element_type=F32)
                wr2 = lax.dot_general(wv, cl, (((1,), (1,)), ((), ())), preferred_element_type=F32)
                cur = (both[:, :NC] + both[:, NC:] + low, wr[0:1] + wr[1:2] + wr2[0:1])
                acc = cur if acc is None else (acc[0] + cur[0], acc[1] + cur[1])
            first = (q * N_PROW + prow) * B + 128 * j - (T + pcol * NC)
            value = matern(gx - cx, gy - cy) + jnp.where(wl_ == ws_ + first, nugget, 0.0) - acc[0]
            slab_ref[q, 128 * j:128 * j + 128, :] = jnp.where(panel, 0.0, value)
            zr = z_ref[pl.ds(jnp.minimum(prow, 1) * 4 + j, 1), :]
            flat_ref[pl.ds(4 * q + j, 1), :] = jnp.where(panel, zr, flat_ref[pl.ds(4 * q + j, 1), :] - acc[1])
        return carry
    lax.fori_loop(0, TILES, body, 0)
    for r in range(32):
        white_ref[r // 4:r // 4 + 1, 128 * (r % 4):128 * (r % 4) + 128] = flat_ref[r:r + 1, :]


def main_call(length_scale, nugget, coords, observations, sites, columns):
    vm = pl.BlockSpec(memory_space=pltpu.VMEM)
    sm = pl.BlockSpec(memory_space=pltpu.SMEM)
    return pl.pallas_call(
        main_kernel,
        out_shape=(jax.ShapeDtypeStruct((TILES, B, NC), F32),
                   jax.ShapeDtypeStruct((TILES, B), F32),
                   jax.ShapeDtypeStruct((1, 128), F32)),
        in_specs=[sm, sm, vm, vm, vm, vm], out_specs=(vm, vm, vm),
        scratch_shapes=[
            pltpu.VMEM((NK, NB, WIDTH), F32),
            pltpu.VMEM((NK, NB, NB), F32),
            pltpu.VMEM((NK, NB, NB), F32),
            pltpu.VMEM((NK, NB, T), BF16),
            pltpu.VMEM((NK, NB, T), BF16),
            pltpu.VMEM((NK, NB, 2 * NC), F32),
            pltpu.VMEM((NK, NB), F32),
            pltpu.VMEM((T, 2 * NC), F32),
            pltpu.VMEM((TILES * B, 128), F32),
            pltpu.VMEM((TILES * B, 128), F32),
            pltpu.VMEM((T, 2 * NC), BF16),
            pltpu.VMEM((16, T), BF16),
            pltpu.VMEM((8, 128), F32),
            pltpu.VMEM((32, 128), F32),
            pltpu.VMEM((NB, NB), F32),
        ],
        compiler_params=pltpu.CompilerParams(vmem_limit_bytes=60 * 1024 * 1024),
        name="factor_and_slab",
    )(length_scale, nugget, coords, observations, sites, columns)


def shards(coords, observations, length_scale, nugget):
    sites, columns = gather_sites(coords, observations)
    slab, white, ll = main_call(length_scale, nugget, coords, observations, sites, columns)
    return slab, white, ll[0, :1]


def solution(mesh):
    placed = (P(None, None, "prow"), P(None, "prow"), P(), P())
    return jax.shard_map(
        shards,
        mesh=mesh,
        in_specs=placed,
        out_specs=(P(None, "prow", "pcol"), P(None, "prow"), P()),
        check_vma=False,
    )
```

```python
import math

import jax
import jax.numpy as jnp
from jax import lax
from jax.experimental import pallas as pl
from jax.experimental.pallas import tpu as pltpu
from jax.sharding import PartitionSpec as P

SQRT_THREE = math.sqrt(3.0)
MINUS_LOG2E = -math.log2(math.e)
F32 = jnp.float32
BF16 = jnp.bfloat16
MESH = pl.DeviceIdType.MESH

B = 512
T = 2 * B
NB = 128
SP = 64
PW = 16
NK = T // NB
N_PROW = 16
HALF = 8
TILES = 8
NC = 128
WIDTH = T + 2 * NC


def gather_kernel(co_ref, ob_ref, t_ref, c_ref, xy0, xy1, xyc, ob0, ob1,
                  send_sem, relay_sem, recv_sem, own_sem):
    prow = lax.axis_index("prow")
    pcol = lax.axis_index("pcol")
    half = prow // HALF
    local = prow % HALF
    line = (pcol // 4) * 4
    zlo = pcol % 4
    near = line + jnp.where(zlo < 2, 3, 0)
    feeds = jnp.where(zlo == 3, 0, 2)
    feeder = (half == 0) & ((zlo == 0) | (zlo == 3))
    owners = (0, 1, 2 + pcol // 4)

    def part(z):
        return pl.ds(pl.multiple_of(z * NC, NC), NC)

    def pieces(slot, z):
        if slot == 2:
            return ((co_ref.at[:, 0:1, part(z)], xyc.at[:, 0:1, :]),)
        xy, ob = ((xy0, ob0), (xy1, ob1))[slot]
        return ((co_ref.at[:, 0:1, :], xy.at[:, 0:1, :]), (ob_ref.at[0:1, :], ob.at[0:1, :]))

    barrier = pltpu.get_barrier_semaphore()
    for slot, owner in enumerate(owners):
        @pl.when(local != owner)
        def _():
            pl.semaphore_signal(barrier, inc=1, device_id=(half * HALF + owner, pcol),
                                device_id_type=MESH)

        @pl.when((local == owner) & (half == 1))
        def _():
            pl.semaphore_signal(barrier, inc=1, device_id=(owner, near), device_id_type=MESH)

    def remote(slot, piece, src, dst, sem, target):
        return pltpu.make_async_remote_copy(
            src_ref=src, dst_ref=dst, send_sem=sem, recv_sem=recv_sem.at[slot, piece],
            device_id=target, device_id_type=MESH)

    def spread(slot, owner, from_slot):
        out = []
        for step in range(1, HALF):
            target = (half * HALF + (local + step) % HALF, pcol)
            for n, (src, dst) in enumerate(pieces(slot, zlo)):
                out.append(remote(slot, n, dst if from_slot else src, dst,
                                  send_sem.at[step, n], target))
        return out

    def feed(slot):
        out = []
        for e in range(2):
            target = (prow + HALF, line + feeds + e)
            for n, (src, dst) in enumerate(pieces(slot, feeds + e)):
                out.append(remote(slot, n, src, dst, relay_sem.at[e, n], target))
        return out

    for slot, owner in enumerate(owners):
        @pl.when((local == owner) & (half == 0))
        def _():
            @pl.when(feeder)
            def _():
                pl.semaphore_wait(barrier, HALF + 1)
                for c in feed(slot):
                    c.start()

            @pl.when(jnp.logical_not(feeder))
            def _():
                pl.semaphore_wait(barrier, HALF - 1)
            for c in spread(slot, owner, False):
                c.start()
            mine = [pltpu.make_async_copy(src, dst, own_sem.at[n])
                    for n, (src, dst) in enumerate(pieces(slot, zlo))]
            for c in mine:
                c.start()
            for c in mine:
                c.wait()
            for c in spread(slot, owner, False):
                c.wait_send()

            @pl.when(feeder)
            def _():
                for c in feed(slot):
                    c.wait_send()

        @pl.when((local == owner) & (half == 1))
        def _():
            pl.semaphore_wait(barrier, HALF - 1)
            copies = spread(slot, owner, True)
            for c in copies[:len(pieces(slot, zlo))]:
                c.wait_recv()
            for c in copies:
                c.start()
            for c in copies:
                c.wait_send()

    for slot, owner in enumerate(owners):
        @pl.when(local != owner)
        def _():
            for c in spread(slot, owner, False)[:len(pieces(slot, zlo))]:
                c.wait_recv()
    for slot, (xy, ob) in enumerate(((xy0, ob0), (xy1, ob1))):
        at = slice(slot * B, slot * B + B)
        t_ref[0:1, at] = xy[0, 0:1, :]
        t_ref[1:2, at] = xy[1, 0:1, :]
        t_ref[2:3, at] = ob[0:1, :]
    c_ref[0:1, :] = xyc[0, 0:1, :]
    c_ref[1:2, :] = xyc[1, 0:1, :]


def gather_sites(coords, observations):
    vm = pl.BlockSpec(memory_space=pltpu.VMEM)
    stay = pl.BlockSpec(memory_space=pl.ANY)
    return pl.pallas_call(
        gather_kernel,
        out_shape=(jax.ShapeDtypeStruct((4, T), F32), jax.ShapeDtypeStruct((4, NC), F32)),
        in_specs=[stay, stay], out_specs=(vm, vm),
        scratch_shapes=[
            pltpu.VMEM((2, 8, B), F32), pltpu.VMEM((2, 8, B), F32), pltpu.VMEM((2, 8, NC), F32),
            pltpu.VMEM((8, B), F32), pltpu.VMEM((8, B), F32),
            pltpu.SemaphoreType.DMA((HALF, 2)), pltpu.SemaphoreType.DMA((2, 2)),
            pltpu.SemaphoreType.DMA((3, 2)), pltpu.SemaphoreType.DMA((2,)),
        ],
        compiler_params=pltpu.CompilerParams(collective_id=0, has_side_effects=True),
        name="gather_sites",
    )(coords, observations)


def split(x):
    high = x.astype(BF16)
    return high, (x - high.astype(F32)).astype(BF16)


def matern(dx, dy):
    s = 1.0 / lax.rsqrt(dx * dx + dy * dy)
    return (1.0 + s) * jnp.exp2(s * MINUS_LOG2E)


def lanes(x, j):
    return jnp.broadcast_to(x[:, j:j + 1], (8, 128))


def rows(x, i):
    return jnp.take_along_axis(x, jnp.full((8, 128), i, jnp.int32), axis=0)


def mm(x, y):
    return lax.dot_general(x, y, (((1,), (0,)), ((), ())), preferred_element_type=F32)


def mm3(x, y):
    xh, xl = split(x)
    yh, yl = split(y)
    return mm(jnp.concatenate([xh, xh, xl], 1), jnp.concatenate([yh, yl, yh], 0))


def factor_block(d_ref, w_ref, k):
    lane = lax.broadcasted_iota(jnp.int32, (8, 128), 1)
    sub = lax.broadcasted_iota(jnp.int32, (8, 128), 0)
    wide = lax.broadcasted_iota(jnp.int32, (SP, 128), 1)
    nv = SP // 8
    logs = jnp.zeros((8, 128), F32)
    for p in range(NB // SP):
        r0 = SP * p
        a = [d_ref[r0 + 8 * i:r0 + 8 * i + 8, :] for i in range(nv)]
        d = [jnp.ones((8, 128), F32) for _ in range(nv)]
        for c0 in range(0, SP, PW):
            own = range(c0 // 8, (c0 + PW) // 8)
            cols = {(t, v): lanes(a[v], r0 + t)
                    for t in range(c0, c0 + PW) for v in range(t // 8, nv)}
            group = (lane >= r0 + c0) & (lane < r0 + c0 + PW)
            for v in range(c0 // 8, nv):
                fill = jnp.where((lane - r0) == (sub + 8 * v), 1.0, 0.0) if v in own else 0.0
                a[v] = jnp.where(group, fill, a[v])
            for t in range(c0, c0 + PW):
                vt, st = t // 8, t % 8
                pivot = rows(cols[t, vt], st)
                d[vt] = jnp.where(sub == st, pivot, d[vt])
                rp = 1.0 / pivot
                m = {v: cols[t, v] * rp for v in range(vt, nv)}
                for i in range(t + 1, c0 + PW):
                    entry = rows(cols[t, i // 8], i % 8)
                    for v in range(i // 8, nv):
                        if i == t + 1 and v == i // 8:
                            cols[i, v] = cols[i, v] - (cols[t, v] * entry) * rp
                        else:
                            cols[i, v] = cols[i, v] - m[v] * entry
                row = rows(a[vt], st)
                for v in range(vt, nv):
                    mv = jnp.where(sub > st, m[v], 0.0) if v == vt else m[v]
                    a[v] = a[v] - mv * row
        y_out = []
        for v in range(nv):
            y = a[v] * lax.rsqrt(d[v])
            logs = logs + jnp.log(d[v])
            y_out.append(jnp.where((lane > r0 + 8 * v + sub) & (lane < r0 + SP), 0.0, y))
        y = jnp.concatenate(y_out, 0)
        w_ref[k, r0:r0 + SP, :] = jnp.where(wide < r0 + SP, y, 0.0)
        if r0 + SP < NB:
            yh, yl = split(y)
            left = jnp.concatenate([yh.astype(F32), yh.astype(F32), yl.astype(F32)], 0).T
            left = left[r0 + SP:, :].astype(BF16)
            update = mm(left, jnp.concatenate([yh, yl, yh], 0))
            rest = d_ref[r0 + SP:, :]
            own = lax.broadcasted_iota(jnp.int32, rest.shape, 1)
            own = (own >= r0) & (own < r0 + SP)
            d_ref[r0 + SP:, :] = jnp.where(own, 0.0, rest) - update
    return logs


def main_kernel(ls_ref, ng_ref, co_ref, ob_ref, t_ref, c_ref,
                slab_ref, white_ref, ll_ref,
                a_ref, w_ref, wt_ref, yh_ref, yl_ref, yb_ref, z_ref, m_ref,
                rx_ref, ry_ref, mc_ref, wv_ref, ld_ref, flat_ref, d_ref, px_ref, py_ref, fx_ref, fy_ref):
    prow = lax.axis_index("prow")
    pcol = lax.axis_index("pcol")
    rate = SQRT_THREE / jnp.full((1, 128), ls_ref[0], F32)
    nugget = ng_ref[0]
    lane = lax.broadcasted_iota(jnp.int32, (8, 128), 1)
    sub = lax.broadcasted_iota(jnp.int32, (8, 128), 0)
    rate_t = jnp.concatenate([rate] * 8, 1)
    tx = t_ref[0:1, :] * rate_t
    ty = t_ref[1:2, :] * rate_t
    cx = c_ref[0:1, :] * rate
    cy = c_ref[1:2, :] * rate
    ux = [tx[:, 128 * i:128 * i + 128] for i in range(8)] + [cx]
    uy = [ty[:, 128 * i:128 * i + 128] for i in range(8)] + [cy]

    for q in range(TILES):
        for i in range(4):
            at = slice(4 * q + i, 4 * q + i + 1)
            part = slice(128 * i, 128 * i + 128)
            flat_ref[at, :] = ob_ref[q:q + 1, part]
            fx_ref[at, :] = co_ref[0, q:q + 1, part] * rate
            fy_ref[at, :] = co_ref[1, q:q + 1, part] * rate

    def spread_tile(slot, q):
        for i in range(4):
            part = slice(128 * i, 128 * i + 128)
            rx_ref[slot, part, :] = jnp.broadcast_to(fx_ref[pl.ds(4 * q + i, 1), :], (128, 128)).T
            ry_ref[slot, part, :] = jnp.broadcast_to(fy_ref[pl.ds(4 * q + i, 1), :], (128, 128)).T

    wide = lax.broadcasted_iota(jnp.int32, (128, 128), 1)
    for k in range(NK):
        part = slice(128 * k, 128 * k + 128)
        px_ref[part, :] = jnp.broadcast_to(tx[:, part], (128, 128)).T
        py_ref[part, :] = jnp.broadcast_to(ty[:, part], (128, 128)).T
        a_ref[k, :, T + NC:] = jnp.where(
            wide == 0, jnp.broadcast_to(t_ref[2:3, part], (128, 128)).T, 0.0)
    spread_tile(0, 0)
    for k in range(NK):
        def build(g, carry, k=k):
            for e in range(4):
                r = pl.multiple_of(32 * g + 8 * e, 8)
                gx = px_ref[pl.ds(128 * k + r, 8), :]
                gy = py_ref[pl.ds(128 * k + r, 8), :]
                for j in range(k, 9):
                    v = matern(gx - ux[j], gy - uy[j])
                    if j == k:
                        v = v + jnp.where(lane == sub + r, nugget, 0.0)
                    a_ref[k, pl.ds(r, 8), 128 * j:128 * j + 128] = v
            return carry
        lax.fori_loop(0, 4, build, 0)

    ld_ref[...] = jnp.zeros((8, 128), F32)

    def step(k, carry):
        off = pl.ds(pl.multiple_of(128 * k, 128), 128)

        d_ref[...] = a_ref[k, :, off]
        ld_ref[...] = ld_ref[...] + factor_block(d_ref, w_ref, k)
        for kk in range(NK):
            @pl.when(k == kk)
            def _():
                o = 128 * (kk + 1)
                n = WIDTH - o
                w = w_ref[kk]
                wt_ref[kk] = w.T
                y = mm3(w, a_ref[kk, :, o:])
                yh, yl = split(y)
                if kk < NK - 1:
                    yh_ref[kk, :, o:T] = yh[:, :n - 256]
                    yl_ref[kk, :, o:T] = yl[:, :n - 256]
                yb_ref[kk] = y[:, n - 256:]
                z_ref[kk:kk + 1, :] = y[:, n - 128:].T[0:1, :]
                ycat = jnp.concatenate([yh, yl, yh], 0)
                for i in range(kk + 1, NK):
                    f = 128 * (i - kk - 1)
                    th, tl = split(y[:, f:f + 128].T)
                    tcat = jnp.concatenate([th, th, tl], 1)
                    a_ref[i, :, 128 * i:] = a_ref[i, :, 128 * i:] - mm(tcat, ycat[:, f:])
        return carry
    lax.fori_loop(0, NK, step, 0)

    for k in range(NK - 1, -1, -1):
        acc = yb_ref[k]
        if k < NK - 1:
            o = 128 * (k + 1)
            mh, ml = split(m_ref[o:, :])
            yh = yh_ref[k, :, o:T]
            acc = acc - (mm(yh, mh) + mm(yh, ml) + mm(yl_ref[k, :, o:T], mh))
        m_ref[128 * k:128 * k + 128, :] = mm3(wt_ref[k], acc)

    mh, ml = split(m_ref[:, :NC])
    mc_ref[:T, :NC] = mh
    mc_ref[:T, NC:] = ml
    mc_ref[T:, :NC] = mh
    mc_ref[T:, NC:] = jnp.zeros((T, NC), BF16)
    wt = m_ref[:, NC:].T
    wh, wl = split(wt[0:1, :])
    wv_ref[...] = jnp.concatenate([wh, wl, jnp.zeros((14, T), BF16)], 0)

    z = z_ref[...]
    total = jnp.sum(z * z) + jnp.sum(ld_ref[:, 0:1])
    ll_ref[...] = jnp.full((1, 128), total * (-0.5 / T), F32)

    ws_ = lax.broadcasted_iota(jnp.int32, (128, 128), 0)

    def body(q, carry):
        panel = (q == 0) & (prow < 2)
        slot = q % 2
        spread_tile(1 - slot, jnp.minimum(q + 1, TILES - 1))
        for j in range(4):
            rows_j = slice(128 * j, 128 * j + 128)
            gx = rx_ref[slot, rows_j, :]
            gy = ry_ref[slot, rows_j, :]
            high, low = [], []
            for t in range(8):
                ch, cl = split(matern(gx - ux[t], gy - uy[t]))
                high.append(ch)
                low.append(cl)
            ch = jnp.concatenate(high, 1)
            cl = jnp.concatenate(low, 1)
            both = mm(jnp.concatenate([ch, cl], 1), mc_ref[...])
            nt = (((1,), (1,)), ((), ()))
            wr = lax.dot_general(wv_ref[...], ch, nt, preferred_element_type=F32)
            wr2 = lax.dot_general(wv_ref[...], cl, nt, preferred_element_type=F32)
            first = (q * N_PROW + prow) * B + 128 * j - (T + pcol * NC)
            value = matern(gx - cx, gy - cy) + jnp.where(wide == ws_ + first, nugget, 0.0)
            value = value - both[:, :NC] - both[:, NC:]
            slab_ref[q, rows_j, :] = jnp.where(panel, 0.0, value)
            zr = z_ref[pl.ds(jnp.minimum(prow, 1) * 4 + j, 1), :]
            at = pl.ds(4 * q + j, 1)
            flat_ref[at, :] = jnp.where(panel, zr, flat_ref[at, :] - (wr[0:1] + wr[1:2] + wr2[0:1]))
        return carry
    lax.fori_loop(0, TILES, body, 0)
    for r in range(32):
        white_ref[r // 4:r // 4 + 1, 128 * (r % 4):128 * (r % 4) + 128] = flat_ref[r:r + 1, :]


def main_call(length_scale, nugget, coords, observations, sites, columns):
    vm = pl.BlockSpec(memory_space=pltpu.VMEM)
    sm = pl.BlockSpec(memory_space=pltpu.SMEM)
    return pl.pallas_call(
        main_kernel,
        out_shape=(jax.ShapeDtypeStruct((TILES, B, NC), F32),
                   jax.ShapeDtypeStruct((TILES, B), F32),
                   jax.ShapeDtypeStruct((1, 128), F32)),
        in_specs=[sm, sm, vm, vm, vm, vm], out_specs=(vm, vm, vm),
        scratch_shapes=[
            pltpu.VMEM((NK, NB, WIDTH), F32),
            pltpu.VMEM((NK, NB, NB), F32),
            pltpu.VMEM((NK, NB, NB), F32),
            pltpu.VMEM((NK, NB, T), BF16),
            pltpu.VMEM((NK, NB, T), BF16),
            pltpu.VMEM((NK, NB, 2 * NC), F32),
            pltpu.VMEM((NK, NB), F32),
            pltpu.VMEM((T, 2 * NC), F32),
            pltpu.VMEM((2, B, 128), F32),
            pltpu.VMEM((2, B, 128), F32),
            pltpu.VMEM((2 * T, 2 * NC), BF16),
            pltpu.VMEM((16, T), BF16),
            pltpu.VMEM((8, 128), F32),
            pltpu.VMEM((32, 128), F32),
            pltpu.VMEM((NB, NB), F32),
            pltpu.VMEM((T, 128), F32),
            pltpu.VMEM((T, 128), F32),
            pltpu.VMEM((32, 128), F32),
            pltpu.VMEM((32, 128), F32),
        ],
        compiler_params=pltpu.CompilerParams(vmem_limit_bytes=60 * 1024 * 1024),
        name="factor_and_slab",
    )(length_scale, nugget, coords, observations, sites, columns)


def shards(coords, observations, length_scale, nugget):
    sites, columns = gather_sites(coords, observations)
    slab, white, ll = main_call(length_scale, nugget, coords, observations, sites, columns)
    return slab, white, ll[0, :1]


def solution(mesh):
    placed = (P(None, None, "prow"), P(None, "prow"), P(), P())
    return jax.shard_map(
        shards,
        mesh=mesh,
        in_specs=placed,
        out_specs=(P(None, "prow", "pcol"), P(None, "prow"), P()),
        check_vma=False,
    )
```

```python
import math

import jax
import jax.numpy as jnp
from jax import lax
from jax.experimental import pallas as pl
from jax.experimental.pallas import tpu as pltpu
from jax.sharding import PartitionSpec as P

SQRT_THREE = math.sqrt(3.0)
MINUS_LOG2E = -math.log2(math.e)
F32 = jnp.float32
BF16 = jnp.bfloat16
MESH = pl.DeviceIdType.MESH

B = 512
T = 2 * B
NB = 128
SP = 32
PW = 16
NK = T // NB
N_PROW = 16
HALF = 8
TILES = 8
NC = 128
WIDTH = T + 2 * NC


def gather_kernel(co_ref, ob_ref, t_ref, c_ref, xy0, xy1, xyc, ob0, ob1,
                  send_sem, relay_sem, recv_sem, own_sem):
    prow = lax.axis_index("prow")
    pcol = lax.axis_index("pcol")
    half = prow // HALF
    local = prow % HALF
    line = (pcol // 4) * 4
    zlo = pcol % 4
    near = line + jnp.where(zlo < 2, 3, 0)
    feeds = jnp.where(zlo == 3, 0, 2)
    feeder = (half == 0) & ((zlo == 0) | (zlo == 3))
    owners = (0, 1, 2 + pcol // 4)

    def part(z):
        return pl.ds(pl.multiple_of(z * NC, NC), NC)

    def pieces(slot, z):
        if slot == 2:
            return ((co_ref.at[:, 0:1, part(z)], xyc.at[:, 0:1, :]),)
        xy, ob = ((xy0, ob0), (xy1, ob1))[slot]
        return ((co_ref.at[:, 0:1, :], xy.at[:, 0:1, :]), (ob_ref.at[0:1, :], ob.at[0:1, :]))

    barrier = pltpu.get_barrier_semaphore()
    for slot, owner in enumerate(owners):
        @pl.when(local != owner)
        def _():
            pl.semaphore_signal(barrier, inc=1, device_id=(half * HALF + owner, pcol),
                                device_id_type=MESH)

        @pl.when((local == owner) & (half == 1))
        def _():
            pl.semaphore_signal(barrier, inc=1, device_id=(owner, near), device_id_type=MESH)

    def remote(slot, piece, src, dst, sem, target):
        return pltpu.make_async_remote_copy(
            src_ref=src, dst_ref=dst, send_sem=sem, recv_sem=recv_sem.at[slot, piece],
            device_id=target, device_id_type=MESH)

    def spread(slot, owner, from_slot):
        out = []
        for step in range(1, HALF):
            target = (half * HALF + (local + step) % HALF, pcol)
            for n, (src, dst) in enumerate(pieces(slot, zlo)):
                out.append(remote(slot, n, dst if from_slot else src, dst,
                                  send_sem.at[step, n], target))
        return out

    def feed(slot):
        out = []
        for e in range(2):
            target = (prow + HALF, line + feeds + e)
            for n, (src, dst) in enumerate(pieces(slot, feeds + e)):
                out.append(remote(slot, n, src, dst, relay_sem.at[e, n], target))
        return out

    for slot, owner in enumerate(owners):
        @pl.when((local == owner) & (half == 0))
        def _():
            @pl.when(feeder)
            def _():
                pl.semaphore_wait(barrier, HALF + 1)
                for c in feed(slot):
                    c.start()

            @pl.when(jnp.logical_not(feeder))
            def _():
                pl.semaphore_wait(barrier, HALF - 1)
            for c in spread(slot, owner, False):
                c.start()
            mine = [pltpu.make_async_copy(src, dst, own_sem.at[n])
                    for n, (src, dst) in enumerate(pieces(slot, zlo))]
            for c in mine:
                c.start()
            for c in mine:
                c.wait()
            for c in spread(slot, owner, False):
                c.wait_send()

            @pl.when(feeder)
            def _():
                for c in feed(slot):
                    c.wait_send()

        @pl.when((local == owner) & (half == 1))
        def _():
            pl.semaphore_wait(barrier, HALF - 1)
            copies = spread(slot, owner, True)
            for c in copies[:len(pieces(slot, zlo))]:
                c.wait_recv()
            for c in copies:
                c.start()
            for c in copies:
                c.wait_send()

    for slot, owner in enumerate(owners):
        @pl.when(local != owner)
        def _():
            for c in spread(slot, owner, False)[:len(pieces(slot, zlo))]:
                c.wait_recv()
    for slot, (xy, ob) in enumerate(((xy0, ob0), (xy1, ob1))):
        at = slice(slot * B, slot * B + B)
        t_ref[0:1, at] = xy[0, 0:1, :]
        t_ref[1:2, at] = xy[1, 0:1, :]
        t_ref[2:3, at] = ob[0:1, :]
    c_ref[0:1, :] = xyc[0, 0:1, :]
    c_ref[1:2, :] = xyc[1, 0:1, :]


def gather_sites(coords, observations):
    vm = pl.BlockSpec(memory_space=pltpu.VMEM)
    stay = pl.BlockSpec(memory_space=pl.ANY)
    return pl.pallas_call(
        gather_kernel,
        out_shape=(jax.ShapeDtypeStruct((4, T), F32), jax.ShapeDtypeStruct((4, NC), F32)),
        in_specs=[stay, stay], out_specs=(vm, vm),
        scratch_shapes=[
            pltpu.VMEM((2, 8, B), F32), pltpu.VMEM((2, 8, B), F32), pltpu.VMEM((2, 8, NC), F32),
            pltpu.VMEM((8, B), F32), pltpu.VMEM((8, B), F32),
            pltpu.SemaphoreType.DMA((HALF, 2)), pltpu.SemaphoreType.DMA((2, 2)),
            pltpu.SemaphoreType.DMA((3, 2)), pltpu.SemaphoreType.DMA((2,)),
        ],
        compiler_params=pltpu.CompilerParams(collective_id=0, has_side_effects=True),
        name="gather_sites",
    )(coords, observations)


def split(x):
    high = x.astype(BF16)
    return high, (x - high.astype(F32)).astype(BF16)


def matern(dx, dy):
    s = 1.0 / lax.rsqrt(dx * dx + dy * dy)
    return (1.0 + s) * jnp.exp2(s * MINUS_LOG2E)


def lanes(x, j):
    return jnp.broadcast_to(x[:, j:j + 1], (8, 128))


def rows(x, i):
    return jnp.take_along_axis(x, jnp.full((8, 128), i, jnp.int32), axis=0)


def mm(x, y):
    return lax.dot_general(x, y, (((1,), (0,)), ((), ())), preferred_element_type=F32)


def mm3(x, y):
    xh, xl = split(x)
    yh, yl = split(y)
    return mm(jnp.concatenate([xh, xh, xl], 1), jnp.concatenate([yh, yl, yh], 0))


def factor_block(d_ref, w_ref, k):
    lane = lax.broadcasted_iota(jnp.int32, (8, 128), 1)
    sub = lax.broadcasted_iota(jnp.int32, (8, 128), 0)
    wide = lax.broadcasted_iota(jnp.int32, (SP, 128), 1)
    nv = SP // 8
    logs = jnp.zeros((8, 128), F32)
    for p in range(NB // SP):
        r0 = SP * p
        a = [d_ref[r0 + 8 * i:r0 + 8 * i + 8, :] for i in range(nv)]
        d = [jnp.ones((8, 128), F32) for _ in range(nv)]
        for c0 in range(0, SP, PW):
            own = range(c0 // 8, (c0 + PW) // 8)
            cols = {(t, v): lanes(a[v], r0 + t)
                    for t in range(c0, c0 + PW) for v in range(t // 8, nv)}
            group = (lane >= r0 + c0) & (lane < r0 + c0 + PW)
            for v in range(c0 // 8, nv):
                fill = jnp.where((lane - r0) == (sub + 8 * v), 1.0, 0.0) if v in own else 0.0
                a[v] = jnp.where(group, fill, a[v])
            for t in range(c0, c0 + PW, 2):
                vt, st = t // 8, t % 8
                p0 = rows(cols[t, vt], st)
                side = rows(cols[t, vt], st + 1)
                det = p0 * rows(cols[t + 1, vt], st + 1) - side * side
                inv0 = 1.0 / p0
                inv1 = p0 * (1.0 / det)
                d[vt] = jnp.where(sub == st, p0, jnp.where(sub == st + 1, det * inv0, d[vt]))
                m0 = {v: cols[t, v] * inv0 for v in range(vt, nv)}
                for v in range(vt, nv):
                    cols[t + 1, v] = cols[t + 1, v] - m0[v] * side
                m1 = {v: cols[t + 1, v] * inv1 for v in range(vt, nv)}
                for i in range(t + 2, c0 + PW):
                    e0 = rows(cols[t, i // 8], i % 8)
                    e1 = rows(cols[t + 1, i // 8], i % 8)
                    for v in range(i // 8, nv):
                        cols[i, v] = (cols[i, v] - m0[v] * e0) - m1[v] * e1
                for step, m in ((st, m0), (st + 1, m1)):
                    row = rows(a[vt], step)
                    for v in range(vt, nv):
                        mv = jnp.where(sub > step, m[v], 0.0) if v == vt else m[v]
                        a[v] = a[v] - mv * row
        y_out = []
        for v in range(nv):
            y = a[v] * lax.rsqrt(d[v])
            logs = logs + jnp.log(d[v])
            y_out.append(jnp.where((lane > r0 + 8 * v + sub) & (lane < r0 + SP), 0.0, y))
        y = jnp.concatenate(y_out, 0)
        w_ref[k, r0:r0 + SP, :] = jnp.where(wide < r0 + SP, y, 0.0)
        if r0 + SP < NB:
            yh, yl = split(y)
            update = lax.dot_general(
                jnp.concatenate([yh, yh, yl], 0), jnp.concatenate([yh, yl, yh], 0),
                (((0,), (0,)), ((), ())), preferred_element_type=F32)[r0 + SP:, :]
            rest = d_ref[r0 + SP:, :]
            own = lax.broadcasted_iota(jnp.int32, rest.shape, 1)
            own = (own >= r0) & (own < r0 + SP)
            d_ref[r0 + SP:, :] = jnp.where(own, 0.0, rest) - update
    return logs


def main_kernel(ls_ref, ng_ref, co_ref, ob_ref, t_ref, c_ref,
                slab_ref, white_ref, ll_ref,
                a_ref, w_ref, wt_ref, yh_ref, yl_ref, yb_ref, z_ref, m_ref,
                rx_ref, ry_ref, mc_ref, wv_ref, ld_ref, flat_ref, d_ref, px_ref, py_ref, fx_ref, fy_ref):
    prow = lax.axis_index("prow")
    pcol = lax.axis_index("pcol")
    rate = SQRT_THREE / jnp.full((1, 128), ls_ref[0], F32)
    nugget = ng_ref[0]
    lane = lax.broadcasted_iota(jnp.int32, (8, 128), 1)
    sub = lax.broadcasted_iota(jnp.int32, (8, 128), 0)
    rate_t = jnp.concatenate([rate] * 8, 1)
    tx = t_ref[0:1, :] * rate_t
    ty = t_ref[1:2, :] * rate_t
    cx = c_ref[0:1, :] * rate
    cy = c_ref[1:2, :] * rate
    ux = [tx[:, 128 * i:128 * i + 128] for i in range(8)] + [cx]
    uy = [ty[:, 128 * i:128 * i + 128] for i in range(8)] + [cy]

    for q in range(TILES):
        for i in range(4):
            at = slice(4 * q + i, 4 * q + i + 1)
            part = slice(128 * i, 128 * i + 128)
            flat_ref[at, :] = ob_ref[q:q + 1, part]
            fx_ref[at, :] = co_ref[0, q:q + 1, part] * rate
            fy_ref[at, :] = co_ref[1, q:q + 1, part] * rate

    def spread_tile(slot, q):
        for i in range(4):
            part = slice(128 * i, 128 * i + 128)
            rx_ref[slot, part, :] = jnp.broadcast_to(fx_ref[pl.ds(4 * q + i, 1), :], (128, 128)).T
            ry_ref[slot, part, :] = jnp.broadcast_to(fy_ref[pl.ds(4 * q + i, 1), :], (128, 128)).T

    wide = lax.broadcasted_iota(jnp.int32, (128, 128), 1)
    for k in range(NK):
        part = slice(128 * k, 128 * k + 128)
        px_ref[part, :] = jnp.broadcast_to(tx[:, part], (128, 128)).T
        py_ref[part, :] = jnp.broadcast_to(ty[:, part], (128, 128)).T
        a_ref[k, :, T + NC:] = jnp.where(
            wide == 0, jnp.broadcast_to(t_ref[2:3, part], (128, 128)).T, 0.0)
    spread_tile(0, 0)
    for k in range(NK):
        def build(g, carry, k=k):
            for e in range(4):
                r = pl.multiple_of(32 * g + 8 * e, 8)
                gx = px_ref[pl.ds(128 * k + r, 8), :]
                gy = py_ref[pl.ds(128 * k + r, 8), :]
                for j in range(k, 9):
                    v = matern(gx - ux[j], gy - uy[j])
                    if j == k:
                        v = v + jnp.where(lane == sub + r, nugget, 0.0)
                    a_ref[k, pl.ds(r, 8), 128 * j:128 * j + 128] = v
            return carry
        lax.fori_loop(0, 4, build, 0)

    ld_ref[...] = jnp.zeros((8, 128), F32)

    def step(k, carry):
        off = pl.ds(pl.multiple_of(128 * k, 128), 128)

        d_ref[...] = a_ref[k, :, off]
        ld_ref[...] = ld_ref[...] + factor_block(d_ref, w_ref, k)
        for kk in range(NK):
            @pl.when(k == kk)
            def _():
                o = 128 * (kk + 1)
                n = WIDTH - o
                w = w_ref[kk]
                wt_ref[kk] = w.T
                y = mm3(w, a_ref[kk, :, o:])
                yh, yl = split(y)
                if kk < NK - 1:
                    yh_ref[kk, :, o:T] = yh[:, :n - 256]
                    yl_ref[kk, :, o:T] = yl[:, :n - 256]
                yb_ref[kk] = y[:, n - 256:]
                z_ref[kk:kk + 1, :] = y[:, n - 128:].T[0:1, :]
                ycat = jnp.concatenate([yh, yl, yh], 0)
                for i in range(kk + 1, NK):
                    f = 128 * (i - kk - 1)
                    th, tl = split(y[:, f:f + 128].T)
                    tcat = jnp.concatenate([th, th, tl], 1)
                    a_ref[i, :, 128 * i:] = a_ref[i, :, 128 * i:] - mm(tcat, ycat[:, f:])
        return carry
    lax.fori_loop(0, NK, step, 0)

    for k in range(NK - 1, -1, -1):
        acc = yb_ref[k]
        if k < NK - 1:
            o = 128 * (k + 1)
            mh, ml = split(m_ref[o:, :])
            yh = yh_ref[k, :, o:T]
            acc = acc - (mm(yh, mh) + mm(yh, ml) + mm(yl_ref[k, :, o:T], mh))
        m_ref[128 * k:128 * k + 128, :] = mm3(wt_ref[k], acc)

    mh, ml = split(m_ref[:, :NC])
    mc_ref[:T, :NC] = mh
    mc_ref[:T, NC:] = ml
    mc_ref[T:, :NC] = mh
    mc_ref[T:, NC:] = jnp.zeros((T, NC), BF16)
    wt = m_ref[:, NC:].T
    wh, wl = split(wt[0:1, :])
    wv_ref[...] = jnp.concatenate([wh, wl, jnp.zeros((14, T), BF16)], 0)

    z = z_ref[...]
    total = jnp.sum(z * z) + jnp.sum(ld_ref[:, 0:1])
    ll_ref[...] = jnp.full((1, 128), total * (-0.5 / T), F32)

    ws_ = lax.broadcasted_iota(jnp.int32, (128, 128), 0)

    def body(q, carry):
        panel = (q == 0) & (prow < 2)
        slot = q % 2
        spread_tile(1 - slot, jnp.minimum(q + 1, TILES - 1))
        for j in range(4):
            rows_j = slice(128 * j, 128 * j + 128)
            gx = rx_ref[slot, rows_j, :]
            gy = ry_ref[slot, rows_j, :]
            high, low = [], []
            for t in range(8):
                ch, cl = split(matern(gx - ux[t], gy - uy[t]))
                high.append(ch)
                low.append(cl)
            ch = jnp.concatenate(high, 1)
            cl = jnp.concatenate(low, 1)
            both = mm(jnp.concatenate([ch, cl], 1), mc_ref[...])
            nt = (((1,), (1,)), ((), ()))
            wr = lax.dot_general(wv_ref[...], ch, nt, preferred_element_type=F32)
            wr2 = lax.dot_general(wv_ref[...], cl, nt, preferred_element_type=F32)
            first = (q * N_PROW + prow) * B + 128 * j - (T + pcol * NC)
            value = matern(gx - cx, gy - cy) + jnp.where(wide == ws_ + first, nugget, 0.0)
            value = value - both[:, :NC] - both[:, NC:]
            slab_ref[q, rows_j, :] = jnp.where(panel, 0.0, value)
            zr = z_ref[pl.ds(jnp.minimum(prow, 1) * 4 + j, 1), :]
            at = pl.ds(4 * q + j, 1)
            flat_ref[at, :] = jnp.where(panel, zr, flat_ref[at, :] - (wr[0:1] + wr[1:2] + wr2[0:1]))
        return carry
    lax.fori_loop(0, TILES, body, 0)
    for r in range(32):
        white_ref[r // 4:r // 4 + 1, 128 * (r % 4):128 * (r % 4) + 128] = flat_ref[r:r + 1, :]


def main_call(length_scale, nugget, coords, observations, sites, columns):
    vm = pl.BlockSpec(memory_space=pltpu.VMEM)
    sm = pl.BlockSpec(memory_space=pltpu.SMEM)
    return pl.pallas_call(
        main_kernel,
        out_shape=(jax.ShapeDtypeStruct((TILES, B, NC), F32),
                   jax.ShapeDtypeStruct((TILES, B), F32),
                   jax.ShapeDtypeStruct((1, 128), F32)),
        in_specs=[sm, sm, vm, vm, vm, vm], out_specs=(vm, vm, vm),
        scratch_shapes=[
            pltpu.VMEM((NK, NB, WIDTH), F32),
            pltpu.VMEM((NK, NB, NB), F32),
            pltpu.VMEM((NK, NB, NB), F32),
            pltpu.VMEM((NK, NB, T), BF16),
            pltpu.VMEM((NK, NB, T), BF16),
            pltpu.VMEM((NK, NB, 2 * NC), F32),
            pltpu.VMEM((NK, NB), F32),
            pltpu.VMEM((T, 2 * NC), F32),
            pltpu.VMEM((2, B, 128), F32),
            pltpu.VMEM((2, B, 128), F32),
            pltpu.VMEM((2 * T, 2 * NC), BF16),
            pltpu.VMEM((16, T), BF16),
            pltpu.VMEM((8, 128), F32),
            pltpu.VMEM((32, 128), F32),
            pltpu.VMEM((NB, NB), F32),
            pltpu.VMEM((T, 128), F32),
            pltpu.VMEM((T, 128), F32),
            pltpu.VMEM((32, 128), F32),
            pltpu.VMEM((32, 128), F32),
        ],
        compiler_params=pltpu.CompilerParams(vmem_limit_bytes=60 * 1024 * 1024),
        name="factor_and_slab",
    )(length_scale, nugget, coords, observations, sites, columns)


def shards(coords, observations, length_scale, nugget):
    sites, columns = gather_sites(coords, observations)
    slab, white, ll = main_call(length_scale, nugget, coords, observations, sites, columns)
    return slab, white, ll[0, :1]


def solution(mesh):
    placed = (P(None, None, "prow"), P(None, "prow"), P(), P())
    return jax.shard_map(
        shards,
        mesh=mesh,
        in_specs=placed,
        out_specs=(P(None, "prow", "pcol"), P(None, "prow"), P()),
        check_vma=False,
    )
```

```python
import math

import jax
import jax.numpy as jnp
from jax import lax
from jax.experimental import pallas as pl
from jax.experimental.pallas import tpu as pltpu
from jax.sharding import PartitionSpec as P

SQRT_THREE = math.sqrt(3.0)
MINUS_LOG2E = -math.log2(math.e)
F32 = jnp.float32
BF16 = jnp.bfloat16
MESH = pl.DeviceIdType.MESH

B = 512
T = 2 * B
NB = 128
SP = 32
PW = 16
NK = T // NB
N_PROW = 16
HALF = 8
TILES = 8
NC = 128
WIDTH = T + 2 * NC


def gather_kernel(co_ref, ob_ref, t_ref, c_ref, xy0, xy1, xyc, ob0, ob1,
                  send_sem, relay_sem, recv_sem, own_sem):
    prow = lax.axis_index("prow")
    pcol = lax.axis_index("pcol")
    half = prow // HALF
    local = prow % HALF
    line = (pcol // 4) * 4
    zlo = pcol % 4
    near = line + jnp.where(zlo < 2, 3, 0)
    feeds = jnp.where(zlo == 3, 0, 2)
    feeder = (half == 0) & ((zlo == 0) | (zlo == 3))
    owners = (0, 1, 2 + pcol // 4)

    def part(z):
        return pl.ds(pl.multiple_of(z * NC, NC), NC)

    def pieces(slot, z):
        if slot == 2:
            return ((co_ref.at[:, 0:1, part(z)], xyc.at[:, 0:1, :]),)
        xy, ob = ((xy0, ob0), (xy1, ob1))[slot]
        return ((co_ref.at[:, 0:1, :], xy.at[:, 0:1, :]), (ob_ref.at[0:1, :], ob.at[0:1, :]))

    barrier = pltpu.get_barrier_semaphore()
    for slot, owner in enumerate(owners):
        @pl.when(local != owner)
        def _():
            pl.semaphore_signal(barrier, inc=1, device_id=(half * HALF + owner, pcol),
                                device_id_type=MESH)

        @pl.when((local == owner) & (half == 1))
        def _():
            pl.semaphore_signal(barrier, inc=1, device_id=(owner, near), device_id_type=MESH)

    def remote(slot, piece, src, dst, sem, target):
        return pltpu.make_async_remote_copy(
            src_ref=src, dst_ref=dst, send_sem=sem, recv_sem=recv_sem.at[slot, piece],
            device_id=target, device_id_type=MESH)

    def spread(slot, owner, from_slot):
        out = []
        for step in range(1, HALF):
            target = (half * HALF + (local + step) % HALF, pcol)
            for n, (src, dst) in enumerate(pieces(slot, zlo)):
                out.append(remote(slot, n, dst if from_slot else src, dst,
                                  send_sem.at[step, n], target))
        return out

    def feed(slot):
        out = []
        for e in range(2):
            target = (prow + HALF, line + feeds + e)
            for n, (src, dst) in enumerate(pieces(slot, feeds + e)):
                out.append(remote(slot, n, src, dst, relay_sem.at[e, n], target))
        return out

    for slot, owner in enumerate(owners):
        @pl.when((local == owner) & (half == 0))
        def _():
            @pl.when(feeder)
            def _():
                pl.semaphore_wait(barrier, HALF + 1)
                for c in feed(slot):
                    c.start()

            @pl.when(jnp.logical_not(feeder))
            def _():
                pl.semaphore_wait(barrier, HALF - 1)
            for c in spread(slot, owner, False):
                c.start()
            mine = [pltpu.make_async_copy(src, dst, own_sem.at[n])
                    for n, (src, dst) in enumerate(pieces(slot, zlo))]
            for c in mine:
                c.start()
            for c in mine:
                c.wait()
            for c in spread(slot, owner, False):
                c.wait_send()

            @pl.when(feeder)
            def _():
                for c in feed(slot):
                    c.wait_send()

        @pl.when((local == owner) & (half == 1))
        def _():
            pl.semaphore_wait(barrier, HALF - 1)
            copies = spread(slot, owner, True)
            for c in copies[:len(pieces(slot, zlo))]:
                c.wait_recv()
            for c in copies:
                c.start()
            for c in copies:
                c.wait_send()

    for slot, owner in enumerate(owners):
        @pl.when(local != owner)
        def _():
            for c in spread(slot, owner, False)[:len(pieces(slot, zlo))]:
                c.wait_recv()
    for slot, (xy, ob) in enumerate(((xy0, ob0), (xy1, ob1))):
        at = slice(slot * B, slot * B + B)
        t_ref[0:1, at] = xy[0, 0:1, :]
        t_ref[1:2, at] = xy[1, 0:1, :]
        t_ref[2:3, at] = ob[0:1, :]
    c_ref[0:1, :] = xyc[0, 0:1, :]
    c_ref[1:2, :] = xyc[1, 0:1, :]


def gather_sites(coords, observations):
    vm = pl.BlockSpec(memory_space=pltpu.VMEM)
    stay = pl.BlockSpec(memory_space=pl.ANY)
    return pl.pallas_call(
        gather_kernel,
        out_shape=(jax.ShapeDtypeStruct((4, T), F32), jax.ShapeDtypeStruct((4, NC), F32)),
        in_specs=[stay, stay], out_specs=(vm, vm),
        scratch_shapes=[
            pltpu.VMEM((2, 8, B), F32), pltpu.VMEM((2, 8, B), F32), pltpu.VMEM((2, 8, NC), F32),
            pltpu.VMEM((8, B), F32), pltpu.VMEM((8, B), F32),
            pltpu.SemaphoreType.DMA((HALF, 2)), pltpu.SemaphoreType.DMA((2, 2)),
            pltpu.SemaphoreType.DMA((3, 2)), pltpu.SemaphoreType.DMA((2,)),
        ],
        compiler_params=pltpu.CompilerParams(collective_id=0, has_side_effects=True),
        name="gather_sites",
    )(coords, observations)


def split(x):
    high = x.astype(BF16)
    return high, (x - high.astype(F32)).astype(BF16)


def matern(dx, dy):
    s = 1.0 / lax.rsqrt(dx * dx + dy * dy)
    return (1.0 + s) * jnp.exp2(s * MINUS_LOG2E)


def lanes(x, j):
    return jnp.broadcast_to(x[:, j:j + 1], (8, 128))


def rows(x, i):
    return jnp.take_along_axis(x, jnp.full((8, 128), i, jnp.int32), axis=0)


def mm(x, y):
    return lax.dot_general(x, y, (((1,), (0,)), ((), ())), preferred_element_type=F32)


def mm3(x, y):
    xh, xl = split(x)
    yh, yl = split(y)
    return mm(jnp.concatenate([xh, xh, xl], 1), jnp.concatenate([yh, yl, yh], 0))


def factor_block(d_ref, w_ref, k):
    lane = lax.broadcasted_iota(jnp.int32, (8, 128), 1)
    sub = lax.broadcasted_iota(jnp.int32, (8, 128), 0)
    wide = lax.broadcasted_iota(jnp.int32, (SP, 128), 1)
    nv = SP // 8
    logs = jnp.zeros((8, 128), F32)
    for p in range(NB // SP):
        r0 = SP * p
        a = [d_ref[r0 + 8 * i:r0 + 8 * i + 8, :] for i in range(nv)]
        d = [jnp.ones((8, 128), F32) for _ in range(nv)]
        for c0 in range(0, SP, PW):
            own = range(c0 // 8, (c0 + PW) // 8)
            cols = {(t, v): lanes(a[v], r0 + t)
                    for t in range(c0, c0 + PW) for v in range(t // 8, nv)}
            group = (lane >= r0 + c0) & (lane < r0 + c0 + PW)
            for v in range(c0 // 8, nv):
                fill = jnp.where((lane - r0) == (sub + 8 * v), 1.0, 0.0) if v in own else 0.0
                a[v] = jnp.where(group, fill, a[v])
            for t in range(c0, c0 + PW, 2):
                vt, st = t // 8, t % 8
                p0 = rows(cols[t, vt], st)
                side = rows(cols[t, vt], st + 1)
                det = p0 * rows(cols[t + 1, vt], st + 1) - side * side
                inv0 = 1.0 / p0
                inv1 = p0 * (1.0 / det)
                d[vt] = jnp.where(sub == st, p0, jnp.where(sub == st + 1, det * inv0, d[vt]))
                m0 = {v: cols[t, v] * inv0 for v in range(vt, nv)}
                for v in range(vt, nv):
                    cols[t + 1, v] = cols[t + 1, v] - m0[v] * side
                m1 = {v: cols[t + 1, v] * inv1 for v in range(vt, nv)}
                for i in range(t + 2, c0 + PW):
                    e0 = rows(cols[t, i // 8], i % 8)
                    e1 = rows(cols[t + 1, i // 8], i % 8)
                    for v in range(i // 8, nv):
                        cols[i, v] = (cols[i, v] - m0[v] * e0) - m1[v] * e1
                for step, m in ((st, m0), (st + 1, m1)):
                    row = rows(a[vt], step)
                    for v in range(vt, nv):
                        mv = jnp.where(sub > step, m[v], 0.0) if v == vt else m[v]
                        a[v] = a[v] - mv * row
        y_out = []
        for v in range(nv):
            y = a[v] * lax.rsqrt(d[v])
            logs = logs + jnp.log(d[v])
            y_out.append(jnp.where((lane > r0 + 8 * v + sub) & (lane < r0 + SP), 0.0, y))
        y = jnp.concatenate(y_out, 0)
        w_ref[k, r0:r0 + SP, :] = jnp.where(wide < r0 + SP, y, 0.0)
        if r0 + SP < NB:
            yh, yl = split(y)
            update = lax.dot_general(
                jnp.concatenate([yh, yh, yl], 0), jnp.concatenate([yh, yl, yh], 0),
                (((0,), (0,)), ((), ())), preferred_element_type=F32)[r0 + SP:, :]
            rest = d_ref[r0 + SP:, :]
            own = lax.broadcasted_iota(jnp.int32, rest.shape, 1)
            own = (own >= r0) & (own < r0 + SP)
            d_ref[r0 + SP:, :] = jnp.where(own, 0.0, rest) - update
    return logs


def main_kernel(ls_ref, ng_ref, co_ref, ob_ref, t_ref, c_ref,
                slab_ref, white_ref, ll_ref,
                a_ref, w_ref, wt_ref, yh_ref, yl_ref, yb_ref, z_ref, m_ref,
                rx_ref, ry_ref, mc_ref, wv_ref, ld_ref, flat_ref, d_ref, px_ref, py_ref, fx_ref, fy_ref):
    prow = lax.axis_index("prow")
    pcol = lax.axis_index("pcol")
    rate = SQRT_THREE / jnp.full((1, 128), ls_ref[0], F32)
    nugget = ng_ref[0]
    lane = lax.broadcasted_iota(jnp.int32, (8, 128), 1)
    sub = lax.broadcasted_iota(jnp.int32, (8, 128), 0)
    rate_t = jnp.concatenate([rate] * 8, 1)
    tx = t_ref[0:1, :] * rate_t
    ty = t_ref[1:2, :] * rate_t
    cx = c_ref[0:1, :] * rate
    cy = c_ref[1:2, :] * rate
    ux = [tx[:, 128 * i:128 * i + 128] for i in range(8)] + [cx]
    uy = [ty[:, 128 * i:128 * i + 128] for i in range(8)] + [cy]

    for q in range(TILES):
        for i in range(4):
            at = slice(4 * q + i, 4 * q + i + 1)
            part = slice(128 * i, 128 * i + 128)
            flat_ref[at, :] = ob_ref[q:q + 1, part]
            fx_ref[at, :] = co_ref[0, q:q + 1, part] * rate
            fy_ref[at, :] = co_ref[1, q:q + 1, part] * rate

    def spread_tile(slot, q):
        for i in range(4):
            part = slice(128 * i, 128 * i + 128)
            rx_ref[slot, part, :] = jnp.broadcast_to(fx_ref[pl.ds(4 * q + i, 1), :], (128, 128)).T
            ry_ref[slot, part, :] = jnp.broadcast_to(fy_ref[pl.ds(4 * q + i, 1), :], (128, 128)).T

    wide = lax.broadcasted_iota(jnp.int32, (128, 128), 1)
    for k in range(NK):
        part = slice(128 * k, 128 * k + 128)
        px_ref[part, :] = jnp.broadcast_to(tx[:, part], (128, 128)).T
        py_ref[part, :] = jnp.broadcast_to(ty[:, part], (128, 128)).T
        a_ref[k, :, T + NC:] = jnp.where(
            wide == 0, jnp.broadcast_to(t_ref[2:3, part], (128, 128)).T, 0.0)
    spread_tile(0, 0)
    spread_tile(1, 1)
    for k in range(NK):
        def build(g, carry, k=k):
            for e in range(4):
                r = pl.multiple_of(32 * g + 8 * e, 8)
                gx = px_ref[pl.ds(128 * k + r, 8), :]
                gy = py_ref[pl.ds(128 * k + r, 8), :]
                for j in range(k, 9):
                    v = matern(gx - ux[j], gy - uy[j])
                    if j == k:
                        v = v + jnp.where(lane == sub + r, nugget, 0.0)
                    a_ref[k, pl.ds(r, 8), 128 * j:128 * j + 128] = v
            return carry
        lax.fori_loop(0, 4, build, 0)

    ld_ref[...] = jnp.zeros((8, 128), F32)

    def step(k, carry):
        off = pl.ds(pl.multiple_of(128 * k, 128), 128)

        d_ref[...] = a_ref[k, :, off]
        ld_ref[...] = ld_ref[...] + factor_block(d_ref, w_ref, k)
        for kk in range(NK):
            @pl.when(k == kk)
            def _():
                o = 128 * (kk + 1)
                n = WIDTH - o
                w = w_ref[kk]
                wt_ref[kk] = w.T
                y = mm3(w, a_ref[kk, :, o:])
                yh, yl = split(y)
                if kk < NK - 1:
                    yh_ref[kk, :, o:T] = yh[:, :n - 256]
                    yl_ref[kk, :, o:T] = yl[:, :n - 256]
                yb_ref[kk] = y[:, n - 256:]
                z_ref[kk:kk + 1, :] = y[:, n - 128:].T[0:1, :]
                ycat = jnp.concatenate([yh, yl, yh], 0)
                tcat = jnp.concatenate([yh, yh, yl], 0)
                for i in range(kk + 1, NK):
                    f = 128 * (i - kk - 1)
                    a_ref[i, :, 128 * i:] = a_ref[i, :, 128 * i:] - lax.dot_general(
                        tcat[:, f:f + 128], ycat[:, f:], (((0,), (0,)), ((), ())),
                        preferred_element_type=F32)
        return carry
    lax.fori_loop(0, NK, step, 0)

    for k in range(NK - 1, -1, -1):
        acc = yb_ref[k]
        if k < NK - 1:
            o = 128 * (k + 1)
            mh, ml = split(m_ref[o:, :])
            yh = yh_ref[k, :, o:T]
            acc = acc - (mm(yh, mh) + mm(yh, ml) + mm(yl_ref[k, :, o:T], mh))
        m_ref[128 * k:128 * k + 128, :] = mm3(wt_ref[k], acc)

    mh, ml = split(m_ref[:, :NC])
    mc_ref[:T, :NC] = mh
    mc_ref[:T, NC:] = ml
    mc_ref[T:, :NC] = mh
    mc_ref[T:, NC:] = jnp.zeros((T, NC), BF16)
    wt = m_ref[:, NC:].T
    wh, wl = split(wt[0:1, :])
    wv_ref[...] = jnp.concatenate([wh, wl, jnp.zeros((14, T), BF16)], 0)

    z = z_ref[...]
    total = jnp.sum(z * z) + jnp.sum(ld_ref[:, 0:1])
    ll_ref[...] = jnp.full((1, 128), total * (-0.5 / T), F32)

    ws_ = lax.broadcasted_iota(jnp.int32, (128, 128), 0)

    def body(pair, carry):
        for e in range(2):
            q = 2 * pair + e
            panel = (q == 0) & (prow < 2)
            slot = 2 * (pair % 2) + e
            spread_tile(2 * (1 - pair % 2) + e, jnp.minimum(q + 2, TILES - 1))
            for j in range(4):
                rows_j = slice(128 * j, 128 * j + 128)
                gx = rx_ref[slot, rows_j, :]
                gy = ry_ref[slot, rows_j, :]
                high, low = [], []
                for t in range(8):
                    ch, cl = split(matern(gx - ux[t], gy - uy[t]))
                    high.append(ch)
                    low.append(cl)
                ch = jnp.concatenate(high, 1)
                cl = jnp.concatenate(low, 1)
                both = mm(jnp.concatenate([ch, cl], 1), mc_ref[...])
                nt = (((1,), (1,)), ((), ()))
                wr = lax.dot_general(wv_ref[...], ch, nt, preferred_element_type=F32)
                wr2 = lax.dot_general(wv_ref[...], cl, nt, preferred_element_type=F32)
                first = (q * N_PROW + prow) * B + 128 * j - (T + pcol * NC)
                value = matern(gx - cx, gy - cy) + jnp.where(wide == ws_ + first, nugget, 0.0)
                value = value - both[:, :NC] - both[:, NC:]
                slab_ref[q, rows_j, :] = jnp.where(panel, 0.0, value)
                zr = z_ref[pl.ds(jnp.minimum(prow, 1) * 4 + j, 1), :]
                at = pl.ds(4 * q + j, 1)
                flat_ref[at, :] = jnp.where(panel, zr, flat_ref[at, :] - (wr[0:1] + wr[1:2] + wr2[0:1]))
        return carry
    lax.fori_loop(0, TILES // 2, body, 0)
    for r in range(32):
        white_ref[r // 4:r // 4 + 1, 128 * (r % 4):128 * (r % 4) + 128] = flat_ref[r:r + 1, :]


def main_call(length_scale, nugget, coords, observations, sites, columns):
    vm = pl.BlockSpec(memory_space=pltpu.VMEM)
    sm = pl.BlockSpec(memory_space=pltpu.SMEM)
    return pl.pallas_call(
        main_kernel,
        out_shape=(jax.ShapeDtypeStruct((TILES, B, NC), F32),
                   jax.ShapeDtypeStruct((TILES, B), F32),
                   jax.ShapeDtypeStruct((1, 128), F32)),
        in_specs=[sm, sm, vm, vm, vm, vm], out_specs=(vm, vm, vm),
        scratch_shapes=[
            pltpu.VMEM((NK, NB, WIDTH), F32),
            pltpu.VMEM((NK, NB, NB), F32),
            pltpu.VMEM((NK, NB, NB), F32),
            pltpu.VMEM((NK, NB, T), BF16),
            pltpu.VMEM((NK, NB, T), BF16),
            pltpu.VMEM((NK, NB, 2 * NC), F32),
            pltpu.VMEM((NK, NB), F32),
            pltpu.VMEM((T, 2 * NC), F32),
            pltpu.VMEM((4, B, 128), F32),
            pltpu.VMEM((4, B, 128), F32),
            pltpu.VMEM((2 * T, 2 * NC), BF16),
            pltpu.VMEM((16, T), BF16),
            pltpu.VMEM((8, 128), F32),
            pltpu.VMEM((32, 128), F32),
            pltpu.VMEM((NB, NB), F32),
            pltpu.VMEM((T, 128), F32),
            pltpu.VMEM((T, 128), F32),
            pltpu.VMEM((32, 128), F32),
            pltpu.VMEM((32, 128), F32),
        ],
        compiler_params=pltpu.CompilerParams(vmem_limit_bytes=60 * 1024 * 1024),
        name="factor_and_slab",
    )(length_scale, nugget, coords, observations, sites, columns)


def shards(coords, observations, length_scale, nugget):
    sites, columns = gather_sites(coords, observations)
    slab, white, ll = main_call(length_scale, nugget, coords, observations, sites, columns)
    return slab, white, ll[0, :1]


def solution(mesh):
    placed = (P(None, None, "prow"), P(None, "prow"), P(), P())
    return jax.shard_map(
        shards,
        mesh=mesh,
        in_specs=placed,
        out_specs=(P(None, "prow", "pcol"), P(None, "prow"), P()),
        check_vma=False,
    )
```
